256 devices in a mesh: tbl: 64 (over z, x, core), hst: 4 (over y).
Axes of the slice: x: 4, y: 4, z: 8, core: 2. Of those that a mesh axis runs over, the one named last changes fastest.
Arguments:
- pooled: bfloat16 [32768, 1024], P('tbl'), may hold values from -16 to 16
- w_up: bfloat16 [1024, 4096], P(None, 'hst'), may hold values from -0.1875 to 0.1875
- grad_out: bfloat16 [32768, 4096], P('tbl', 'hst'), may hold values from -6 to 6
- owners: int32 [8, 32768, 8], P('hst', 'tbl'), may hold values from 0 to 63, all different within a row; in each aligned block of 512 rows (0 to 511, 512 to 1023, ..., all dimensions but the last counted through in order) at most 128 rows name the same one
- rows: int32 [8, 32768, 8], P('hst', 'tbl'), may hold values from 0 to 1023
- lookup_weight: bfloat16 [8, 32768, 8], P('hst', 'tbl'), may hold values from 0.25 to 2
- lens: int32 [8, 32768], P('hst', 'tbl'), may hold values from 4 to 8
- slot_map: int32 [64, 4, 2048], P('tbl', 'hst'), may hold values from 0 to 2047, each once within a row
- cache_weight: float32 [64, 4, 2048, 128], P('tbl', 'hst'), may hold values from -6 to 6
- cache_accum: float32 [64, 4, 2048], P('tbl', 'hst'), may hold values from 0.1 to 10
- evict_slots: int32 [64, 4, 256], P('tbl', 'hst'), may hold values from 0 to 2047, as said below
- evict_dest: int32 [64, 4, 256], P('tbl', 'hst'), may hold values from 0 to 3, as said below
- evict_count: int32 [64, 4], P('tbl', 'hst'), may hold values from 128 to 256
Outputs:
- grad_up: float32 [1024, 4096], P('tbl', 'hst')
- new_weight: float32 [64, 4, 2048, 128], P('tbl', 'hst')
- new_accum: float32 [64, 4, 2048], P('tbl', 'hst')
- held_rows: float32 [64, 4, 4, 128, 128], P('tbl', 'hst')
- held_accum: float32 [64, 4, 4, 128], P('tbl', 'hst')
The draws below stay inside these ranges and needn't reach their ends.
Inputs may be any that keep to these rules, and one draw needn't show every extreme that they name: The 8 owners of one bag differ. Among the 512 samples of one index of tbl and one table, no owner is named by more than 128 lookup positions, used or not; some owner is named by exactly 128 in some such block. `evict_slots`: the 256 slots of one device's list differ. `evict_dest`: among the used entries of one device, no holder appears more than 128 times, and one holder appears exactly 128 times.
All inputs are finite; a program needn't handle non-finite values.
Results may differ from the reference program's by a relative error of at most 0.0029.
Values may be sent and summed in bfloat16 or wider, within the bound.
No kernel may reach another device: no remote copies, remote signals or barrier semaphores. Data moves between devices by JAX's collectives and lax.ppermute only.
A program may use at most 64 MiB of HBM per device.

```python
import math
import jax
import jax.numpy as jnp
import numpy as np
from jax import lax

EMB = 128
HIDDEN_SIZE = 4096
TABLES_DEV = 2
BAG = 8
B_DEV = 512
ROWS_DEV = 1024
EVICT = 256
OWNERS = 64
HOLDERS = 4
B = 32768
TABLES = 8
FEAT = 1024
SLOTS = 2048
CAP = 128
MOST = 128


def eviction_plan(key):
    keys = jax.random.split(jax.random.fold_in(key, 7), 4)
    devices = OWNERS * HOLDERS
    amounts = jax.random.randint(keys[0], (devices,), CAP, EVICT + 1)
    favored = jax.random.randint(keys[1], (devices,), 0, HOLDERS)
    offsets = jax.random.randint(keys[2], (devices, EVICT), 1, HOLDERS)
    positions = jnp.arange(EVICT, dtype=jnp.int32)
    baseline = jnp.where(positions[None, :] < CAP, favored[:, None], (favored[:, None] + offsets) % HOLDERS)
    scores = jax.random.randint(keys[3], (devices, EVICT), 0, 1 << 20)
    sorting = jnp.where(positions[None, :] < amounts[:, None], scores * EVICT + positions[None, :], (1 << 30) + positions[None, :])
    arrange = jnp.argsort(sorting, axis=1, stable=True)
    targets = jnp.take_along_axis(baseline, arrange, axis=1)
    return (targets.reshape(OWNERS, HOLDERS, EVICT).astype(jnp.int32), amounts.reshape(OWNERS, HOLDERS).astype(jnp.int32))


def draw_evict_dest(key, part):
    return eviction_plan(key)[0]


def draw_evict_count(key, part):
    return eviction_plan(key)[1]


def draw_evict_slots(key, part):
    keys = jax.random.split(jax.random.fold_in(key, 11), OWNERS * HOLDERS)
    chosen = jax.vmap(lambda single: jax.random.permutation(single, SLOTS)[:EVICT])(keys)
    return chosen.reshape(OWNERS, HOLDERS, EVICT).astype(jnp.int32)


def plant(array, own_key, low, top_value):
    extent = array.shape
    spot = [jax.random.randint(jax.random.fold_in(own_key, axis), (), 0, extent[axis]) for axis in range(len(extent))]
    array = array.at[tuple(spot)].set(low)
    longest = extent.index(max(extent))
    spot[longest] = (spot[longest] + 1) % extent[longest]
    return array.at[tuple(spot)].set(top_value)


def strengthened(entries, own_key, source, target, blocks, factor):
    def block_of(position):
        return (jnp.arange(entries.shape[position]) // (entries.shape[position] // blocks)).reshape((-1,) + (1,) * (entries.ndim - 1 - position))

    near = jax.random.permutation(own_key, blocks)[block_of(target)]
    second = (block_of(target) + blocks // 2) % blocks
    return jnp.where((block_of(source) == near) | (block_of(source) == second), factor * entries, entries)


def steps_of(stream_key, shape, cuts, smallest, top_value):
    factor_of = 1.0
    for axis_at, blocks in cuts:
        steps = jax.random.uniform(jax.random.fold_in(jax.random.fold_in(stream_key, 6), axis_at), (blocks,), jnp.float32, smallest / len(cuts), top_value / len(cuts))
        factor_of = factor_of * jnp.repeat(jnp.exp(steps), shape[axis_at] // blocks).reshape((-1,) + (1,) * (len(shape) - 1 - axis_at))
    return factor_of


def assign_block(rng, own, number, rows, amount, top, bound, skew):
    sequence = jax.random.permutation(rng, amount)
    heavy_load, usual = shares(amount, rows * top, bound, skew, True), shares(amount, rows * top, bound, skew, False)
    places = jnp.arange(amount)

    def named(lengths, rotation):
        used = int((lengths > 0).sum())
        fixed = max(1, used // 4)
        passed = fixed + (places - fixed + rotation * (used - fixed)) % max(1, amount - fixed)
        return jnp.zeros((amount,), jnp.int32).at[sequence[jnp.where(places < fixed, places, passed)]].set(jnp.asarray(lengths, jnp.int32))

    lengths = jnp.where(number % 4 == 0, named(heavy_load, number // 4), named(usual, number - number // 4 - 1))
    mixed = jax.random.permutation(jax.random.fold_in(own, 3), amount)
    giver, receiver = mixed[0:amount // 2 * 2:2], mixed[1:amount // 2 * 2:2]
    slack = jnp.minimum(lengths[giver] - 1, bound - lengths[receiver]) // 2
    slack = jnp.where((giver == sequence[0]) | (receiver == sequence[0]) | (lengths[receiver] == 0), 0, jnp.maximum(slack, 0))
    passed = jax.random.randint(jax.random.fold_in(own, 4), (amount // 2,), 0, 1 << 20) % (slack + 1)
    lengths = lengths.at[giver].add(-passed).at[receiver].add(passed)
    members = jnp.searchsorted(jnp.cumsum(lengths), jnp.arange(rows * top), side="right").astype(jnp.int32)
    grid = members.reshape(top, rows).T
    grid = grid[jax.random.permutation(jax.random.fold_in(own, 1), rows)]
    rotation = jax.random.randint(jax.random.fold_in(own, 2), (rows, 1), 0, top)
    return jnp.take_along_axis(grid, (jnp.arange(top)[None, :] + rotation) % top, axis=1)


def shares(number_of, total, bound, slope, full):
    portions = [(1 << 20) // math.isqrt(rank ** slope) + 1 for rank in range(1, number_of + 1)]
    largest = bound if full else min(bound, max(-(-total // number_of), total * portions[0] // sum(portions)))
    least = 1 if total - largest >= number_of - 1 else 0
    given, rest = [largest] + [least] * (number_of - 1), total - largest - least * (number_of - 1)
    while rest > 0:
        candidates = [i for i in range(1, number_of) if given[i] < largest] or [i for i in range(1, number_of) if given[i] < bound]
        mass, budget = sum([portions[i] for i in candidates]), rest
        for i in candidates:
            extra = min(bound - given[i], max(1, budget * portions[i] // mass), rest)
            given[i] = given[i] + extra
            rest = rest - extra
    return np.array(given)


def gaussian(key, extent, scale, bound, cuts=(), held_as=jnp.bfloat16):
    values = scale * jax.random.normal(key, extent, jnp.float32)
    if cuts:
        values = values * steps_of(key, extent, cuts, -0.22, 0.18)
    return jnp.clip(values, -bound, bound).astype(held_as)


def bell_draw_with(key, extent, width, limit, cuts, heavy, held_as=jnp.bfloat16):
    result = width * jax.random.normal(key, extent, jnp.float32)
    if cuts:
        result = result * steps_of(key, extent, cuts, -0.22, 0.18)
    return jnp.clip(strengthened(result, jax.random.fold_in(key, 3), *heavy), -limit, limit).astype(held_as)


def setup_inputs(seed: int = 0) -> dict:
    streams_of = jax.random.split(jax.random.key(seed), 14)
    pooled = bell_draw_with(streams_of[0], (B, FEAT), 1.0, 16.0, ((0, 64),), (0, 1, 64, 4.0))
    w_up = gaussian(streams_of[1], (FEAT, HIDDEN_SIZE), FEAT ** -0.5, 0.1875, ((1, 4),))
    grad_out = gaussian(streams_of[2], (B, HIDDEN_SIZE), 1.0, 6.0, ((0, 64), (1, 4)))
    owners_keys = jax.random.split(jax.random.fold_in(streams_of[3], 1), TABLES * B // B_DEV)
    owners_turns = jax.random.permutation(jax.random.fold_in(streams_of[3], 3), TABLES * B // B_DEV)
    owners = jax.vmap(lambda own, number: assign_block(jax.random.fold_in(streams_of[3], 2), own, number, B_DEV, OWNERS, BAG, MOST, 1))(owners_keys, owners_turns).reshape((TABLES, B, BAG))
    rows = plant(jax.random.randint(streams_of[4], (TABLES, B, BAG), 0, ROWS_DEV), jax.random.fold_in(streams_of[4], 1), 0, ROWS_DEV - 1).astype(jnp.int32)
    lookup_weight = jnp.clip(jnp.exp(math.log(2.0) - 2.0794415 * jax.random.uniform(streams_of[5], (TABLES, B, BAG), jnp.float32) ** steps_of(streams_of[5], (TABLES, B, BAG), ((0, 4), (1, 64)), -0.2, 0.2)), 0.25, 2.0).astype(jnp.bfloat16)
    lens = plant(jax.random.randint(streams_of[6], (TABLES, B), (BAG + 1) // 2, BAG + 1), jax.random.fold_in(streams_of[6], 1), (BAG + 1) // 2, BAG).astype(jnp.int32)
    slot_map = jax.vmap(lambda own: jax.random.permutation(own, SLOTS))(jax.random.split(streams_of[7], OWNERS * HOLDERS)).reshape((OWNERS, HOLDERS, SLOTS)).astype(jnp.int32)
    cache_weight = gaussian(streams_of[8], (OWNERS, HOLDERS, SLOTS, EMB), 1.0, 6.0, ((0, 64), (1, 4)), jnp.float32)
    cache_accum = jnp.clip(jnp.exp(math.log(10.0) - 4.6051702 * jax.random.uniform(streams_of[9], (OWNERS, HOLDERS, SLOTS), jnp.float32) ** steps_of(streams_of[9], (OWNERS, HOLDERS, SLOTS), ((0, 64), (1, 4)), -0.2, 0.2)), 0.1, 10.0)
    evict_slots = draw_evict_slots(jax.random.fold_in(streams_of[13], 71), 0)
    evict_dest = draw_evict_dest(jax.random.fold_in(streams_of[13], 71), 0)
    evict_count = draw_evict_count(jax.random.fold_in(streams_of[13], 71), 0)
    return {"pooled": pooled, "w_up": w_up, "grad_out": grad_out, "owners": owners, "rows": rows, "lookup_weight": lookup_weight, "lens": lens, "slot_map": slot_map, "cache_weight": cache_weight, "cache_accum": cache_accum, "evict_slots": evict_slots, "evict_dest": evict_dest, "evict_count": evict_count}


LEARN_RATE = 0.05
EPSILON = 1e-08

def reference(pooled, w_up, grad_out, owners, rows, lookup_weight, lens, slot_map, cache_weight, cache_accum, evict_slots, evict_dest, evict_count):
    preact = jnp.dot(pooled, w_up, preferred_element_type=jnp.float32)
    sigmoid_z = jax.nn.sigmoid(preact)
    delta = (grad_out.astype(jnp.float32) * sigmoid_z * (1.0 + preact * (1.0 - sigmoid_z))).astype(jnp.bfloat16)
    grad_up = lax.dot_general(pooled, delta, (((0,), (0,)), ((), ())), preferred_element_type=jnp.float32)
    feature_grad = lax.dot_general(delta, w_up, (((1,), (1,)), ((), ())), preferred_element_type=jnp.float32)
    bag_grad = feature_grad.astype(jnp.bfloat16).reshape(B, TABLES, EMB)
    bag_major = jnp.transpose(bag_grad, (1, 0, 2)).astype(jnp.float32)
    positions = jnp.arange(BAG, dtype=jnp.int32)
    used = positions[None, None, :] < lens[:, :, None]
    flat_size = OWNERS * HOLDERS * SLOTS

    def one_table(running, table):
        group = table // TABLES_DEV
        local_table = table % TABLES_DEV
        own_rows = owners[table]
        slot_index = slot_map[own_rows, group, local_table * ROWS_DEV + rows[table]]
        flat_index = (own_rows * HOLDERS + group) * SLOTS + slot_index
        flat_index = jnp.where(used[table], flat_index, flat_size).astype(jnp.int32)
        scaled = (lookup_weight[table].astype(jnp.float32)[:, :, None] * bag_major[table][:, None, :]).astype(jnp.bfloat16)
        scaled = lax.optimization_barrier(scaled).astype(jnp.float32)
        running = running.at[flat_index.reshape(-1)].add(scaled.reshape(-1, EMB), mode='drop')
        return (running, None)
    slot_grad, _ = lax.scan(one_table, jnp.zeros((flat_size, EMB), jnp.float32), jnp.arange(TABLES, dtype=jnp.int32))
    slot_grad = slot_grad.reshape(OWNERS, HOLDERS, SLOTS, EMB)
    new_accum = cache_accum + lax.optimization_barrier(jnp.mean(slot_grad * slot_grad, axis=-1))
    new_weight = cache_weight - LEARN_RATE * slot_grad / (jnp.sqrt(new_accum)[..., None] + EPSILON)
    leaving = jnp.take_along_axis(new_weight, evict_slots[..., None], axis=2)
    leaving_accum = jnp.take_along_axis(new_accum, evict_slots, axis=2)
    live = jnp.arange(EVICT, dtype=jnp.int32)[None, None, :] < evict_count[:, :, None]
    picks = ((evict_dest[..., None] == jnp.arange(HOLDERS, dtype=jnp.int32)) & live[..., None]).astype(jnp.int32)
    placed = lax.optimization_barrier(jnp.sum((jnp.cumsum(picks, axis=2) - 1) * picks, axis=-1))
    device_index = jnp.arange(OWNERS, dtype=jnp.int32)[:, None] * HOLDERS + jnp.arange(HOLDERS, dtype=jnp.int32)[None, :]
    goal = device_index[:, :, None] * (HOLDERS * CAP) + evict_dest * CAP + placed
    goal = jnp.where(live, goal, OWNERS * HOLDERS * HOLDERS * CAP).astype(jnp.int32)
    held_flat = jnp.zeros((OWNERS * HOLDERS * HOLDERS * CAP, EMB), jnp.float32).at[goal.reshape(-1)].set(leaving.reshape(-1, EMB), mode='drop')
    accum_flat = jnp.zeros((OWNERS * HOLDERS * HOLDERS * CAP,), jnp.float32).at[goal.reshape(-1)].set(leaving_accum.reshape(-1), mode='drop')
    held_rows = jnp.transpose(held_flat.reshape(OWNERS, HOLDERS, HOLDERS, CAP, EMB), (0, 2, 1, 3, 4))
    held_accum = jnp.transpose(accum_flat.reshape(OWNERS, HOLDERS, HOLDERS, CAP), (0, 2, 1, 3))
    return (grad_up, new_weight, new_accum, held_rows, held_accum)
```

```python
import functools

import jax
import jax.numpy as jnp
from jax import lax
from jax.experimental import pallas as pl
from jax.experimental.pallas import tpu as pltpu
from jax.sharding import Mesh
from jax.sharding import PartitionSpec as P

TBL = ("tbl_0", "tbl_1", "tbl_2")
Z, X, C, H = "tbl_0", "tbl_1", "tbl_2", "hst"

LEARN_RATE = 0.05
EPSILON = 1e-08
F32 = jnp.float32
BF16 = jnp.bfloat16
I32 = jnp.int32
VMEM = pl.BlockSpec(memory_space=pltpu.VMEM)
SMEM = pl.BlockSpec(memory_space=pltpu.SMEM)
MOST = 128
HELD = 136


def shifted(x, axis, step):
    size = lax.axis_size(axis)
    return lax.ppermute(x, axis, [(i, (i + step) % size) for i in range(size)])


def call(body, ins, outs, scratch, flops, moved, name):
    return pl.pallas_call(
        body,
        in_specs=ins,
        out_specs=[VMEM] * len(outs),
        out_shape=outs,
        scratch_shapes=scratch,
        compiler_params=pltpu.CompilerParams(vmem_limit_bytes=48 << 20),
        cost_estimate=pl.CostEstimate(flops=flops, bytes_accessed=moved, transcendentals=0),
        name=name,
    )


def top_kernel(pos, pooled, w_up, grad_out, delta, *parts):
    w = w_up[...]
    half = 256
    for i in range(2):
        at = pl.ds(i * half, half)
        preact = jnp.dot(pooled[at, :], w, preferred_element_type=F32)
        s = jax.nn.sigmoid(preact)
        delta[at, :] = (grad_out[at, :].astype(F32) * s * (1.0 + preact * (1.0 - s))).astype(BF16)
    h = pos[3]
    count = len(parts) // 2
    for k in (2, 1, 3, 0):
        to = lax.rem(h + k, count)
        for t in range(2):
            row = pl.multiple_of(to * 256 + t * 128, 128)
            block = w_up[pl.ds(row, 128), :]
            out = lax.dot_general(
                delta[...], block, (((1,), (1,)), ((), ())), preferred_element_type=F32
            )
            ref = parts[t * count + k]
            ref[...] = out.astype(ref.dtype)


def code_kernel(pos, owner, value, lens, *outs):
    z = pos[0]
    planes = len(outs)
    tables, bag, bags = owner.shape
    lane_owner = lax.broadcasted_iota(I32, (8, bags), 0)
    for t in range(tables):
        used = [jnp.where(l < lens[t : t + 1, :], owner[t, l : l + 1, :], -1) for l in range(bag)]
        vals = [value[t, l : l + 1, :] for l in range(bag)]
        for k in range(planes):
            ids = lane_owner + lax.rem(z + k, planes) * 8
            total = jnp.zeros((8, bags), I32)
            for l in range(bag):
                total = total + jnp.where(used[l] == ids, vals[l], 0)
            outs[k][t] = total


def place_kernel(table, sources, pos, *refs):
    codes, refs = refs[:sources], refs[sources:]
    bags_in, refs = refs[: sources + 1], refs[sources + 1 :]
    keep, send, code_all, rank_all, bag_all, picks, rhs, rows, his, wts, spread = refs
    owners = 8
    bags = code_all.shape[1]
    for s in range(sources):
        code_all[s * owners : (s + 1) * owners, :] = codes[s][table]
    for s in range(sources - 1):
        bag_all[s] = bags_in[s][...]
    bag_all[sources - 1, : bags // 2] = bags_in[sources - 1][...]
    bag_all[sources - 1, bags // 2 :] = bags_in[sources][...]
    earlier = (
        lax.broadcasted_iota(I32, (bags, bags), 0) < lax.broadcasted_iota(I32, (bags, bags), 1)
    )
    earlier = jnp.where(earlier, 1.0, 0.0).astype(BF16)
    present = code_all[...] > 0
    rank = jnp.dot(jnp.where(present, 1.0, 0.0).astype(BF16), earlier, preferred_element_type=F32)
    rank_all[...] = jnp.where(present, rank, 1000.0)
    rhs[:, 128:] = jnp.zeros((bags, 128), BF16)
    place = lax.broadcasted_iota(I32, (MOST, 1), 0).astype(F32)

    def gather(s, carry):
        first = pl.multiple_of(s * owners, owners)
        code = code_all[pl.ds(first, owners), :]
        row = lax.shift_right_logical(code, 11)
        w = (code & 2047).astype(F32) * (1.0 / 512.0)
        fields = [
            lax.shift_right_logical(row, 5).astype(F32),
            (lax.shift_right_logical(row, 1) & 15).astype(F32),
            (row & 1).astype(F32),
            w,
            jnp.zeros((128 - 4 * owners, bags), F32),
        ]
        rhs[:, 128:] = jnp.concatenate(fields, axis=0).T.astype(BF16)
        rhs[:, :128] = bag_all[s]
        rank_s = rank_all[pl.ds(first, owners), :]
        for o in range(owners):
            picks[o * MOST : (o + 1) * MOST, :] = jnp.where(
                rank_s[o : o + 1, :] == place, 1.0, 0.0
            ).astype(BF16)
        for o in range(0, owners, 2):
            got2 = jnp.dot(picks[o * MOST : (o + 2) * MOST, :], rhs[...], preferred_element_type=F32)
            for i in range(2):
                got = got2[i * MOST : (i + 1) * MOST]
                q = o + i
                low = got[:, 128 + 16 + q : 128 + 17 + q]
                vec = got[:, :128]
                at = pl.ds(pl.multiple_of(s * MOST, MOST), MOST)
                rows[q, at, :128] = jnp.where(low == 0.0, vec, 0.0).astype(BF16)
                rows[q, at, 128:] = jnp.where(low == 0.0, 0.0, vec).astype(BF16)
                side = got[:, 128:].T
                his[s, q : q + 1, :] = side[q : q + 1] * 16.0 + side[8 + q : 9 + q]
                wts[s, q : q + 1, :] = side[24 + q : 25 + q]
        return carry

    lax.fori_loop(0, sources, gather, 0)
    x, c = pos[1], pos[2]
    half_rows = lax.broadcasted_iota(I32, (512, 1), 0).astype(F32)

    def spread_owner(k, other):
        o = 2 * lax.rem(x + k, 4) + (c + other) % 2
        for s in range(sources):
            hi = his[s, pl.ds(o, 1), :]
            wt = wts[s, pl.ds(o, 1), :]
            spread[:, s * MOST : (s + 1) * MOST] = jnp.where(hi == half_rows, wt, 0.0).astype(BF16)
        return jnp.dot(spread[...], rows[o], preferred_element_type=F32)

    def send_one(k, carry):
        send[k] = spread_owner(k, 1).astype(BF16)
        return carry

    def keep_one(k, carry):
        keep[k] = spread_owner(k, 0)
        return carry

    lax.fori_loop(0, 4, send_one, 0)
    lax.fori_loop(0, 4, keep_one, 0)


def update_kernel(pos, slots_s, goal_s, count_s, slot_map, weight, accum, *refs):
    parts, refs = refs[:8], refs[8:]
    new_weight, new_accum = refs[:2]
    held, refs = refs[2:6], refs[6:]
    rhs, acc_wide, hold, hold_acc = refs
    for t in range(2):
        own = parts[4 * t][...].astype(F32)
        for k in range(1, 4):
            own = own + parts[4 * t + k][...].astype(F32)
        high = own.astype(BF16)
        low = (own - high.astype(F32)).astype(BF16)
        for l in range(2):
            at = (2 * t + l) * 512
            rhs[at : at + 512, :128] = high[:, l * 128 : (l + 1) * 128]
            rhs[at : at + 512, 128:] = low[:, l * 128 : (l + 1) * 128]
    hold[...] = jnp.zeros_like(hold)
    hold_acc[...] = jnp.zeros_like(hold_acc)
    eye = lax.broadcasted_iota(I32, (128, 128), 0) == lax.broadcasted_iota(I32, (128, 128), 1)
    step = 256
    ids = lax.broadcasted_iota(I32, (step, 1), 0)
    slot_row = slot_map[...]

    def chunk(i, carry):
        at = pl.multiple_of(i * step, step)
        pick = jnp.where(slot_row == ids + at, 1.0, 0.0).astype(BF16)
        both = jnp.dot(pick, rhs[...], preferred_element_type=F32)
        grad = both[:, :128] + both[:, 128:]
        for j in range(step // 128):
            g = grad[j * 128 : (j + 1) * 128]
            b = i * (step // 128) + j
            kept = jnp.sum(jnp.where(eye, accum[pl.ds(b, 1), :], 0.0), axis=1, keepdims=True)
            acc = kept + jnp.sum(g * g, axis=1, keepdims=True) * (1.0 / 128.0)
            wide = jnp.broadcast_to(acc, (128, 128))
            here = pl.ds(pl.multiple_of(at + j * 128, 128), 128)
            acc_wide[here, :] = wide
            new_accum[pl.ds(b, 1), :] = jnp.sum(jnp.where(eye, wide, 0.0), axis=0, keepdims=True)
            new_weight[here, :] = weight[here, :] - LEARN_RATE * g / (jnp.sqrt(acc) + EPSILON)
        return carry

    lax.fori_loop(0, 2048 // step, chunk, 0)

    def leave(p, carry):
        slot, goal = slots_s[p], goal_s[p]
        hold[pl.ds(goal, 1), :] = new_weight[pl.ds(slot, 1), :]
        hold_acc[pl.ds(goal, 1), :] = acc_wide[pl.ds(slot, 1), :]
        return carry

    lax.fori_loop(0, count_s[0], leave, 0)
    for k in range(4):
        held[k][:128, :] = hold[k * 128 : (k + 1) * 128, :]
        line = jnp.sum(jnp.where(eye, hold_acc[k * 128 : (k + 1) * 128, :], 0.0), axis=0, keepdims=True)
        held[k][128:, :] = jnp.broadcast_to(line, (HELD - 128, 128))


def arrive_kernel(pos, b0, b1, b2, b3, rows, accum):
    h = pos[3]
    for k, ref in enumerate((b0, b1, b2, b3)):
        at = lax.rem(h + 4 - k, 4)
        rows[at] = ref[:128, :]
        accum[pl.ds(at, 1), :] = ref[128:129, :]


def on_device(
    pooled,
    w_up,
    grad_out,
    owners,
    rows,
    lookup_weight,
    lens,
    slot_map,
    cache_weight,
    cache_accum,
    evict_slots,
    evict_dest,
    evict_count,
):
    shape = jax.ShapeDtypeStruct
    bags = pooled.shape[0]
    z, x, c, h = (lax.axis_index(a) for a in (Z, X, C, H))
    pos = jnp.stack([z, x, c, h]).astype(I32)

    outs = [shape((bags, 1024), BF16)]
    for t in range(2):
        outs += [shape((bags, 128), F32)] + [shape((bags, 128), BF16)] * 3
    delta, *parts = call(
        top_kernel, [SMEM, VMEM, VMEM, VMEM], outs, [], 2 << 30, 6 << 20, "top"
    )(pos, pooled, w_up, grad_out)

    value = rows * 2048 + (lookup_weight.astype(F32) * 512.0).astype(I32)
    codes_out = call(
        code_kernel, [SMEM, VMEM, VMEM, VMEM], [shape((2, 8, bags), I32)] * 8, [], 1 << 22, 1 << 20, "codes"
    )(pos, jnp.swapaxes(owners, 1, 2), jnp.swapaxes(value, 1, 2), lens)
    codes = [codes_out[0]] + [shifted(codes_out[k], Z, k) for k in range(1, 8)]
    order = (0, 1, 7, 2, 6, 3, 5, 4)

    tables = []
    for t in range(2):
        mine = parts[4 * t]
        got = [shifted(parts[4 * t + k], H, k).astype(F32) for k in (1, 2, 3)]
        tables.append((mine + got[0] + got[1] + got[2]).astype(BF16))
    gathered = []
    for t in range(2):
        own = tables[t]
        up, down, blocks = own, own, [own]
        for _ in range(3):
            up, down = shifted(up, Z, 1), shifted(down, Z, -1)
            blocks += [up, down]
        blocks += [shifted(up[: bags // 2], Z, 1), shifted(down[bags // 2 :], Z, -1)]
        gathered.append(blocks)

    grad = lax.dot_general(pooled, delta, (((0,), (0,)), ((), ())), preferred_element_type=F32)
    grad = grad.reshape(8, 4, 2, 16, 1024)
    there = lax.dynamic_index_in_dim(grad, 1 - c, 2, keepdims=False)
    here = lax.dynamic_index_in_dim(grad, c, 2, keepdims=False)
    grad = here + shifted(there, C, 1)
    total = lax.dynamic_index_in_dim(grad, x, 1, keepdims=False)
    for k in (1, 2, 3):
        block = lax.dynamic_index_in_dim(grad, lax.rem(x + k, 4), 1, keepdims=False)
        total = total + shifted(block.astype(BF16), X, k).astype(F32)
    grad_up = lax.dynamic_index_in_dim(total, z, 0, keepdims=False)
    for k in range(1, 8):
        block = lax.dynamic_index_in_dim(total, lax.rem(z + k, 8), 0, keepdims=False)
        grad_up = grad_up + shifted(block.astype(BF16), Z, k).astype(F32)

    arrived = []
    for t in range(2):
        keep, send = call(
            functools.partial(place_kernel, t, 8),
            [SMEM] + [VMEM] * 17,
            [shape((4, 512, 256), F32), shape((4, 512, 256), BF16)],
            [
                pltpu.VMEM((64, bags), I32),
                pltpu.VMEM((64, bags), F32),
                pltpu.VMEM((8, bags, 128), BF16),
                pltpu.VMEM((8 * MOST, bags), BF16),
                pltpu.VMEM((bags, 256), BF16),
                pltpu.VMEM((8, 8 * MOST, 256), BF16),
                pltpu.VMEM((8, 8, MOST), F32),
                pltpu.VMEM((8, 8, MOST), F32),
                pltpu.VMEM((512, 8 * MOST), BF16),
            ],
            8 << 30,
            8 << 20,
            f"place{t}",
        )(pos, *[codes[k] for k in order], *gathered[t])
        other = shifted(send, C, 1).astype(F32)
        both = [keep[k] + other[k] for k in range(4)]
        arrived += [both[0]] + [shifted(both[k].astype(BF16), X, k) for k in (1, 2, 3)]

    list_len = evict_slots.shape[-1]
    departure = evict_dest[0, 0]
    list_ids = jnp.arange(list_len, dtype=I32)
    live = list_ids < evict_count[0, 0]
    picks = ((departure[:, None] == jnp.arange(4, dtype=I32)) & live[:, None]).astype(BF16)
    before = (list_ids[:, None] > list_ids[None, :]).astype(BF16)
    counted = jnp.dot(before, picks, preferred_element_type=F32)
    placed = jnp.sum(counted * picks.astype(F32), axis=-1).astype(I32)
    goal = lax.rem(departure + 4 - h, 4) * 128 + placed
    slot_rows = jnp.swapaxes(slot_map.reshape(2, 512, 2), 1, 2).reshape(1, 2048)
    new_weight, new_accum, *held = call(
        update_kernel,
        [SMEM] * 4 + [VMEM] * 11,
        [shape((2048, 128), F32), shape((16, 128), F32)] + [shape((HELD, 128), F32)] * 4,
        [
            pltpu.VMEM((2048, 256), BF16),
            pltpu.VMEM((2048, 128), F32),
            pltpu.VMEM((512, 128), F32),
            pltpu.VMEM((512, 128), F32),
        ],
        2 << 30,
        4 << 20,
        "update",
    )(
        pos,
        evict_slots.reshape(-1),
        goal,
        evict_count.reshape(-1),
        slot_rows,
        cache_weight[0, 0],
        cache_accum.reshape(16, 128),
        *arrived,
    )
    held = [held[0]] + [shifted(held[k], H, k) for k in (1, 2, 3)]
    held_rows, held_accum = call(
        arrive_kernel,
        [SMEM] + [VMEM] * 4,
        [shape((4, 128, 128), F32), shape((4, 128), F32)],
        [],
        1 << 10,
        1 << 19,
        "arrive",
    )(pos, *held)
    return (
        grad_up,
        new_weight[None, None],
        new_accum.reshape(1, 1, 2048),
        held_rows[None, None],
        held_accum[None, None],
    )


def solution(mesh):
    torus = Mesh(mesh.devices.reshape(8, 4, 2, mesh.shape["hst"]), (Z, X, C, H))
    in_specs = (
        P(TBL, None),
        P(None, "hst"),
        P(TBL, "hst"),
        P("hst", TBL, None),
        P("hst", TBL, None),
        P("hst", TBL, None),
        P("hst", TBL),
        P(TBL, "hst", None),
        P(TBL, "hst", None, None),
        P(TBL, "hst", None),
        P(TBL, "hst", None),
        P(TBL, "hst", None),
        P(TBL, "hst"),
    )
    out_specs = (
        P(TBL, "hst"),
        P(TBL, "hst", None, None),
        P(TBL, "hst", None),
        P(TBL, "hst", None, None, None),
        P(TBL, "hst", None, None),
    )
    return jax.shard_map(
        on_device, mesh=torus, in_specs=in_specs, out_specs=out_specs, check_vma=False
    )
```

```python
import functools

import jax
import jax.numpy as jnp
from jax import lax
from jax.experimental import pallas as pl
from jax.experimental.pallas import tpu as pltpu
from jax.sharding import Mesh
from jax.sharding import PartitionSpec as P

TBL = ("tbl_0", "tbl_1", "tbl_2")
Z, X, C, H = "tbl_0", "tbl_1", "tbl_2", "hst"

LEARN_RATE = 0.05
EPSILON = 1e-08
F32 = jnp.float32
BF16 = jnp.bfloat16
I32 = jnp.int32
VMEM = pl.BlockSpec(memory_space=pltpu.VMEM)
SMEM = pl.BlockSpec(memory_space=pltpu.SMEM)
MOST = 128
HELD = 136


def shifted(x, axis, step):
    size = lax.axis_size(axis)
    return lax.ppermute(x, axis, [(i, (i + step) % size) for i in range(size)])


def call(body, ins, outs, scratch, flops, moved, name):
    return pl.pallas_call(
        body,
        in_specs=ins,
        out_specs=[VMEM] * len(outs),
        out_shape=outs,
        scratch_shapes=scratch,
        compiler_params=pltpu.CompilerParams(vmem_limit_bytes=48 << 20),
        cost_estimate=pl.CostEstimate(flops=flops, bytes_accessed=moved, transcendentals=0),
        name=name,
    )


def top_kernel(pos, pooled, w_up, grad_out, delta, own, one, two, three, feature):
    width = 256

    def column(i, carry):
        at = pl.ds(pl.multiple_of(i * width, width), width)
        preact = jnp.dot(pooled[...], w_up[:, at], preferred_element_type=F32)
        s = jax.nn.sigmoid(preact)
        delta[:, at] = (grad_out[:, at].astype(F32) * s * (1.0 + preact * (1.0 - s))).astype(BF16)
        return carry

    lax.fori_loop(0, 4, column, 0)
    h = pos[3]

    def part(k, carry):
        row = pl.multiple_of(lax.rem(h + k, 4) * width, width)
        feature[k] = lax.dot_general(
            delta[...],
            w_up[pl.ds(row, width), :],
            (((1,), (1,)), ((), ())),
            preferred_element_type=F32,
        )
        return carry

    lax.fori_loop(0, 4, part, 0)
    bags = delta.shape[0]
    for k, ref in enumerate((own, one, two, three)):
        for t in range(2):
            ref[t * bags : (t + 1) * bags, :] = feature[k, :, t * 128 : (t + 1) * 128].astype(ref.dtype)


def code_kernel(pos, owner, value, lens, out):
    x, c = pos[1], pos[2]
    tables, bag, bags = owner.shape
    j = lax.broadcasted_iota(I32, (8, bags), 0)
    there = 2 * ((x + j) & 3) + ((c + (j >> 2)) & 1)
    for t in range(tables):
        used = [jnp.where(l < lens[t : t + 1, :], owner[t, l : l + 1, :], -1) for l in range(bag)]
        vals = [value[t, l : l + 1, :] for l in range(bag)]
        for k in range(out.shape[0]):
            ids = there + k * 8
            total = jnp.zeros((8, bags), I32)
            for l in range(bag):
                total = total + jnp.where(used[l] == ids, vals[l], 0)
            out[k, 8 * t : 8 * t + 8, :] = total


STEPS = (1, 2, 2, 2, 1)


def prep_kernel(order, pos, codes, *refs):
    ranks, sides, code_all, rank_all = refs[:5], refs[5:10], refs[10], refs[11]
    bags = code_all.shape[1]
    for s in range(8):
        code_all[16 * s : 16 * s + 16, :] = codes[lax.rem(pos[0] + 8 - order[s], 8)]
    earlier = (
        lax.broadcasted_iota(I32, (bags, bags), 0) < lax.broadcasted_iota(I32, (bags, bags), 1)
    )
    earlier = jnp.where(earlier, 1.0, 0.0).astype(BF16)
    present = code_all[...] > 0
    rank = jnp.dot(jnp.where(present, 1.0, 0.0).astype(BF16), earlier, preferred_element_type=F32)
    rank_all[...] = jnp.where(present, rank, 255.0)
    first = 0
    for step, count in enumerate(STEPS):

        def unit(i, carry):
            at = pl.ds(pl.multiple_of((first + i) * 8, 8), 8)
            code = code_all[at, :]
            ranks[step][i] = rank_all[at, :]
            row = lax.shift_right_logical(code, 11)
            fields = [
                lax.shift_right_logical(row, 2).astype(F32),
                (code & 2047).astype(F32) * (1.0 / 512.0),
                (row & 3).astype(F32),
                jnp.zeros((128 - 24, bags), F32),
            ]
            sides[step][i] = jnp.concatenate(fields, axis=0).T.astype(BF16)
            return carry

        lax.fori_loop(0, 2 * count, unit, 0)
        first += 2 * count


def pick_kernel(count, ranks, sides, *refs):
    blocks, refs = refs[:2], refs[2:]
    outs, bag_all, picks, rhs = refs[:12], refs[12], refs[13], refs[14]
    bags = bag_all.shape[2]
    if count == 1:
        for t in range(2):
            bag_all[0, t] = blocks[t][...]
    else:
        for s in range(2):
            for t in range(2):
                bag_all[s, t] = blocks[s][t * bags : (t + 1) * bags, :]
    place = lax.broadcasted_iota(I32, (MOST, bags), 0).astype(F32).astype(BF16)

    def source(s, carry):
        for t in range(2):
            rhs[t, :, :128] = bag_all[s, t]
            rhs[t, :, 128:] = sides[2 * s + t]
            rank = ranks[2 * s + t].astype(BF16)
            for o in range(8):
                line = jnp.broadcast_to(rank[o : o + 1, :], (MOST, bags))
                picks[t, o * MOST : (o + 1) * MOST, :] = jnp.where(
                    line == place, jnp.ones((), BF16), jnp.zeros((), BF16)
                )
        for t in range(2):
            for o in range(0, 8, 2):
                got2 = jnp.dot(
                    picks[t, o * MOST : (o + 2) * MOST, :], rhs[t], preferred_element_type=F32
                )
                for i in range(2):
                    q = o + i
                    got = got2[i * MOST : (i + 1) * MOST]
                    rows, low, meta = outs[3 * (2 * t + q // 4) : 3 * (2 * t + q // 4) + 3]
                    k = q % 4
                    rows[s, k] = got[:, :128].astype(BF16)
                    low[s, k] = jnp.broadcast_to(
                        got[:, 128 + 16 + q : 128 + 17 + q], (MOST, 128)
                    ).astype(BF16)
                    side = got[:, 128:].T
                    meta[s, k : k + 1, :] = side[q : q + 1]
                    meta[s, 4 + k : 5 + k, :] = side[8 + q : 9 + q]
        return carry

    lax.fori_loop(0, count, source, 0)


def spread_one(k, steps, onto, both):
    ids = lax.broadcasted_iota(I32, (256, MOST), 0).astype(F32).astype(BF16)
    s = 0
    for rows, low, meta in steps:
        for i in range(rows.shape[0]):
            at = slice(s * MOST, (s + 1) * MOST)
            high = jnp.broadcast_to(meta[i, pl.ds(k, 1), :].astype(BF16), (256, MOST))
            wt = jnp.broadcast_to(meta[i, pl.ds(k + 4, 1), :].astype(BF16), (256, MOST))
            onto[:, at] = jnp.where(high == ids, wt, jnp.zeros((), BF16))
            vec, bits = rows[i, k], low[i, k]
            for l in range(4):
                both[at, l * 128 : (l + 1) * 128] = jnp.where(
                    bits == jnp.full((), l, BF16), vec, jnp.zeros((), BF16)
                )
            s += 1
    return jnp.dot(onto[...], both[...], preferred_element_type=F32)


def send_kernel(*refs):
    steps = [refs[3 * i : 3 * i + 3] for i in range(5)]
    out, onto, both = refs[15:]

    def one(k, carry):
        out[k] = spread_one(k, steps, onto, both).astype(BF16)
        return carry

    lax.fori_loop(0, 4, one, 0)


def keep_kernel(other, *refs):
    steps = [refs[3 * i : 3 * i + 3] for i in range(5)]
    outs, onto, both, total = refs[15:19], refs[19], refs[20], refs[21]

    def one(k, carry):
        total[k] = spread_one(k, steps, onto, both) + other[k].astype(F32)
        return carry

    lax.fori_loop(0, 4, one, 0)
    for k in range(4):
        outs[k][...] = total[k].astype(outs[k].dtype)


def grad_kernel(pos, pooled, delta, keep, send, half):
    x, c = pos[1], pos[2]

    def piece(i, carry):
        at = pl.ds(pl.multiple_of(i * 512, 512), 512)
        half[...] = lax.dot_general(
            pooled[:, at], delta[...], (((0,), (0,)), ((), ())), preferred_element_type=F32
        )
        for j in range(4):
            kz = i * 4 + j
            for k in range(4):
                row = j * 128 + lax.rem(x + k, 4) * 32
                keep[k, kz] = half[pl.ds(pl.multiple_of(row + c * 16, 16), 16), :]
                send[k, kz] = half[pl.ds(pl.multiple_of(row + (1 - c) * 16, 16), 16), :]
        return carry

    lax.fori_loop(0, 2, piece, 0)


def update_kernel(pos, slots_s, goal_s, slot_map, weight, accum, *refs):
    parts, refs = refs[:8], refs[8:]
    new_weight, new_accum = refs[:2]
    held, refs = refs[2:6], refs[6:]
    rhs, acc_wide, hold, hold_acc = refs
    for t in range(2):
        own = parts[4 * t][...]
        for k in range(1, 4):
            own = own + parts[4 * t + k][...].astype(F32)
        high = own.astype(BF16)
        low = (own - high.astype(F32)).astype(BF16)
        for l in range(4):
            at = (4 * t + l) * 256
            rhs[at : at + 256, :128] = high[:, l * 128 : (l + 1) * 128]
            rhs[at : at + 256, 128:] = low[:, l * 128 : (l + 1) * 128]
    hold[...] = jnp.zeros_like(hold)
    hold_acc[...] = jnp.zeros_like(hold_acc)
    eye = lax.broadcasted_iota(I32, (128, 128), 0) == lax.broadcasted_iota(I32, (128, 128), 1)
    step = 256
    ids = lax.broadcasted_iota(I32, (step, 2048), 0).astype(F32).astype(BF16)
    slot_row = slot_map[...]

    def chunk(i, carry):
        at = pl.multiple_of(i * step, step)
        near = slot_row - at
        near = jnp.where((near >= 0) & (near < step), near, 2 * step).astype(F32).astype(BF16)
        pick = jnp.where(
            jnp.broadcast_to(near, (step, 2048)) == ids, jnp.ones((), BF16), jnp.zeros((), BF16)
        )
        both = jnp.dot(pick, rhs[...], preferred_element_type=F32)
        grad = both[:, :128] + both[:, 128:]
        for j in range(step // 128):
            g = grad[j * 128 : (j + 1) * 128]
            b = i * (step // 128) + j
            kept = jnp.sum(jnp.where(eye, accum[pl.ds(b, 1), :], 0.0), axis=1, keepdims=True)
            acc = kept + jnp.sum(g * g, axis=1, keepdims=True) * (1.0 / 128.0)
            wide = jnp.broadcast_to(acc, (128, 128))
            here = pl.ds(pl.multiple_of(at + j * 128, 128), 128)
            acc_wide[here, :] = wide
            new_accum[pl.ds(b, 1), :] = jnp.sum(jnp.where(eye, wide, 0.0), axis=0, keepdims=True)
            new_weight[here, :] = weight[here, :] - LEARN_RATE * g / (jnp.sqrt(acc) + EPSILON)
        return carry

    lax.fori_loop(0, 2048 // step, chunk, 0)

    def leave(i, carry):
        for j in range(8):
            slot, goal = slots_s[8 * i + j], goal_s[8 * i + j]
            hold[pl.ds(goal, 1), :] = new_weight[pl.ds(slot, 1), :]
            hold_acc[pl.ds(goal, 1), :] = acc_wide[pl.ds(slot, 1), :]
        return carry

    lax.fori_loop(0, slots_s.shape[0] // 8, leave, 0)
    for k in range(4):
        held[k][:128, :] = hold[k * 128 : (k + 1) * 128, :]
        line = jnp.sum(jnp.where(eye, hold_acc[k * 128 : (k + 1) * 128, :], 0.0), axis=0, keepdims=True)
        held[k][128:, :] = jnp.broadcast_to(line, (HELD - 128, 128))


def arrive_kernel(pos, b0, b1, b2, b3, rows, accum):
    h = pos[3]
    for k, ref in enumerate((b0, b1, b2, b3)):
        at = lax.rem(h + 4 - k, 4)
        rows[at] = ref[:128, :]
        accum[pl.ds(at, 1), :] = ref[128:129, :]


def together(*groups):
    flat = [a for g in groups for a in g]
    flat = lax.optimization_barrier(flat)
    out = []
    for g in groups:
        out.append(flat[: len(g)])
        flat = flat[len(g) :]
    return out


def on_device(
    pooled,
    w_up,
    grad_out,
    owners,
    rows,
    lookup_weight,
    lens,
    slot_map,
    cache_weight,
    cache_accum,
    evict_slots,
    evict_dest,
    evict_count,
):
    shape = jax.ShapeDtypeStruct
    bags = pooled.shape[0]
    z, x, c, h = (lax.axis_index(a) for a in (Z, X, C, H))
    pos = jnp.stack([z, x, c, h]).astype(I32)

    delta, *parts = call(
        top_kernel,
        [SMEM, VMEM, VMEM, VMEM],
        [shape((bags, 1024), BF16), shape((2 * bags, 128), F32)] + [shape((2 * bags, 128), BF16)] * 3,
        [pltpu.VMEM((4, bags, 256), F32)],
        2 << 30,
        6 << 20,
        "top",
    )(pos, pooled, w_up, grad_out)
    got = [shifted(parts[k], H, k) for k in (1, 2, 3)]

    (delta,), (owners, rows, lookup_weight, lens) = together(
        (delta,), (owners, rows, lookup_weight, lens)
    )
    value = rows * 2048 + (lookup_weight.astype(F32) * 512.0).astype(I32)
    (codes,) = call(
        code_kernel, [SMEM, VMEM, VMEM, VMEM], [shape((8, 16, bags), I32)], [], 1 << 22, 1 << 20, "codes"
    )(pos, jnp.swapaxes(owners, 1, 2), jnp.swapaxes(value, 1, 2), lens)
    codes = lax.all_to_all(codes, Z, split_axis=0, concat_axis=0, tiled=True)

    got, (codes,) = together(got, (codes,))
    own = parts[0] + got[0].astype(F32) + got[1].astype(F32) + got[2].astype(F32)
    own = own.astype(BF16)
    order = (0, 1, 7, 2, 6, 3, 5, 4)
    units = [2 * n for n in STEPS]
    prep = call(
        functools.partial(prep_kernel, order),
        [SMEM, VMEM],
        [shape((n, 8, bags), F32) for n in units] + [shape((n, bags, 128), BF16) for n in units],
        [pltpu.VMEM((128, bags), I32), pltpu.VMEM((128, bags), F32)],
        1 << 26,
        3 << 20,
        "prep",
    )(pos, codes)

    def pick(step, blocks):
        count = STEPS[step]
        outs = [
            shape((count, 4, MOST, 128), BF16),
            shape((count, 4, MOST, 128), BF16),
            shape((count, 8, 128), F32),
        ] * 4
        return call(
            functools.partial(pick_kernel, count),
            [VMEM] * 4,
            outs,
            [
                pltpu.VMEM((count, 2, bags, 128), BF16),
                pltpu.VMEM((2, 8 * MOST, bags), BF16),
                pltpu.VMEM((2, bags, 256), BF16),
            ],
            1 << 30,
            4 << 20,
            f"pick{step}",
        )(prep[step], prep[5 + step], *blocks)

    up, down = shifted(own, Z, 1), shifted(own, Z, -1)
    (delta,), (own,) = together((delta,), (own,))
    grad, there = call(
        grad_kernel,
        [SMEM, VMEM, VMEM],
        [shape((4, 8, 16, 1024), F32)] * 2,
        [pltpu.VMEM((512, 1024), F32)],
        1 << 30,
        6 << 20,
        "grad",
    )(pos, pooled, delta)
    near = (up, down)
    (up, down), (grad, there) = together((up, down), (grad, there))
    there = shifted(there, C, 1)
    up, down = shifted(up, Z, 1), shifted(down, Z, -1)
    picked = [pick(0, (own[:bags], own[bags:]))]
    mid = (up, down)
    (up, down), near, *picked = together((up, down), near, *picked)
    up, down = shifted(up, Z, 1), shifted(down, Z, -1)
    picked.append(pick(1, near))
    grad_x = grad + there
    total, blocks = grad_x[0], [grad_x[k].astype(BF16) for k in (1, 2, 3)]
    far = (up, down)
    (up, down), mid, (total,), blocks, picked[1] = together((up, down), mid, (total,), blocks, picked[1])
    last = (shifted(up[:bags], Z, 1), shifted(down[bags:], Z, -1))
    got_x = [shifted(blocks[k - 1], X, k) for k in (1, 2, 3)]
    picked.append(pick(2, mid))
    picked.append(pick(3, far))
    picked.append(pick(4, last))

    work = [pltpu.VMEM((256, 8 * MOST), BF16), pltpu.VMEM((8 * MOST, 512), BF16)]
    half = lambda t, side: [a for p in picked for a in p[3 * (2 * t + side) : 3 * (2 * t + side) + 3]]
    others = []
    for t in range(2):
        (out,) = call(
            send_kernel, [VMEM] * 15, [shape((4, 256, 512), BF16)], work, 4 << 30, 5 << 20, f"send{t}"
        )(*half(t, 1))
        others.append(shifted(out, C, 1))
    arrived = []
    for t in range(2):
        outs = call(
            keep_kernel,
            [VMEM] * 16,
            [shape((256, 512), F32)] + [shape((256, 512), BF16)] * 3,
            work + [pltpu.VMEM((4, 256, 512), F32)],
            4 << 30,
            5 << 20,
            f"keep{t}",
        )(others[t], *half(t, 0))
        arrived += [outs[0]] + [shifted(outs[k], X, k) for k in (1, 2, 3)]

    for block in got_x:
        total = total + block.astype(F32)
    keep_now, (total,) = together((arrived[4],), (total,))
    arrived[4] = keep_now[0]
    blocks = lax.all_to_all(total.astype(BF16), Z, split_axis=0, concat_axis=0, tiled=True)
    blocks = jnp.where(jnp.arange(8, dtype=I32)[:, None, None] == z, 0.0, blocks.astype(F32))
    grad_up = lax.dynamic_index_in_dim(total, z, 0, keepdims=False) + blocks.sum(axis=0)
    arrived, (grad_up,) = together(arrived, (grad_up,))

    list_len = evict_slots.shape[-1]
    departure = evict_dest[0, 0]
    list_ids = jnp.arange(list_len, dtype=I32)
    live = list_ids < evict_count[0, 0]
    picks = ((departure[:, None] == jnp.arange(4, dtype=I32)) & live[:, None]).astype(BF16)
    before = (list_ids[:, None] > list_ids[None, :]).astype(BF16)
    counted = jnp.dot(before, picks, preferred_element_type=F32)
    placed = jnp.sum(counted * picks.astype(F32), axis=-1).astype(I32)
    goal = jnp.where(live, lax.rem(departure + 4 - h, 4) * 128 + placed, 512)
    slot_rows = jnp.swapaxes(slot_map.reshape(2, 256, 4), 1, 2).reshape(1, 2048)
    new_weight, new_accum, *held = call(
        update_kernel,
        [SMEM] * 3 + [VMEM] * 11,
        [shape((2048, 128), F32), shape((16, 128), F32)] + [shape((HELD, 128), F32)] * 4,
        [
            pltpu.VMEM((2048, 256), BF16),
            pltpu.VMEM((2048, 128), F32),
            pltpu.VMEM((520, 128), F32),
            pltpu.VMEM((520, 128), F32),
        ],
        2 << 30,
        4 << 20,
        "update",
    )(
        pos,
        evict_slots.reshape(-1),
        goal,
        slot_rows,
        cache_weight[0, 0],
        cache_accum.reshape(16, 128),
        *arrived,
    )
    held = [held[0]] + [shifted(held[k], H, k) for k in (1, 2, 3)]
    held_rows, held_accum = call(
        arrive_kernel,
        [SMEM] + [VMEM] * 4,
        [shape((4, 128, 128), F32), shape((4, 128), F32)],
        [],
        1 << 10,
        1 << 19,
        "arrive",
    )(pos, *held)
    return (
        grad_up,
        new_weight[None, None],
        new_accum.reshape(1, 1, 2048),
        held_rows[None, None],
        held_accum[None, None],
    )


def solution(mesh):
    torus = Mesh(mesh.devices.reshape(8, 4, 2, mesh.shape["hst"]), (Z, X, C, H))
    in_specs = (
        P(TBL, None),
        P(None, "hst"),
        P(TBL, "hst"),
        P("hst", TBL, None),
        P("hst", TBL, None),
        P("hst", TBL, None),
        P("hst", TBL),
        P(TBL, "hst", None),
        P(TBL, "hst", None, None),
        P(TBL, "hst", None),
        P(TBL, "hst", None),
        P(TBL, "hst", None),
        P(TBL, "hst"),
    )
    out_specs = (
        P(TBL, "hst"),
        P(TBL, "hst", None, None),
        P(TBL, "hst", None),
        P(TBL, "hst", None, None, None),
        P(TBL, "hst", None, None),
    )
    return jax.shard_map(
        on_device, mesh=torus, in_specs=in_specs, out_specs=out_specs, check_vma=False
    )
```

```python
import functools

import jax
import jax.numpy as jnp
from jax import lax
from jax.experimental import pallas as pl
from jax.experimental.pallas import tpu as pltpu
from jax.sharding import Mesh
from jax.sharding import PartitionSpec as P

TBL = ("tbl_0", "tbl_1", "tbl_2")
Z, X, C, H = "tbl_0", "tbl_1", "tbl_2", "hst"

LEARN_RATE = 0.05
EPSILON = 1e-08
F32 = jnp.float32
BF16 = jnp.bfloat16
I32 = jnp.int32
VMEM = pl.BlockSpec(memory_space=pltpu.VMEM)
SMEM = pl.BlockSpec(memory_space=pltpu.SMEM)
MOST = 128
HELD = 136


def shifted(x, axis, step):
    size = lax.axis_size(axis)
    return lax.ppermute(x, axis, [(i, (i + step) % size) for i in range(size)])


def call(body, ins, outs, scratch, flops, moved, name):
    return pl.pallas_call(
        body,
        in_specs=ins,
        out_specs=[VMEM] * len(outs),
        out_shape=outs,
        scratch_shapes=scratch,
        compiler_params=pltpu.CompilerParams(vmem_limit_bytes=20 << 20),
        cost_estimate=pl.CostEstimate(flops=flops, bytes_accessed=moved, transcendentals=0),
        name=name,
    )


def top_kernel(pos, pooled, w_up, grad_out, delta, own, one, two, three, feature):
    width = 256

    def column(i, carry):
        at = pl.ds(pl.multiple_of(i * width, width), width)
        preact = jnp.dot(pooled[...], w_up[:, at], preferred_element_type=F32)
        s = jax.nn.sigmoid(preact)
        delta[:, at] = (grad_out[:, at].astype(F32) * s * (1.0 + preact * (1.0 - s))).astype(BF16)
        return carry

    lax.fori_loop(0, 4, column, 0)
    h = pos[3]

    def part(k, carry):
        row = pl.multiple_of(lax.rem(h + k, 4) * width, width)
        feature[k] = lax.dot_general(
            delta[...],
            w_up[pl.ds(row, width), :],
            (((1,), (1,)), ((), ())),
            preferred_element_type=F32,
        )
        return carry

    lax.fori_loop(0, 4, part, 0)
    bags = delta.shape[0]
    for k, ref in enumerate((own, one, two, three)):
        for t in range(2):
            ref[t * bags : (t + 1) * bags, :] = feature[k, :, t * 128 : (t + 1) * 128].astype(ref.dtype)


def code_kernel(pos, owner, value, lens, out):
    x, c = pos[1], pos[2]
    tables, bag, bags = owner.shape
    j = lax.broadcasted_iota(I32, (8, bags), 0)
    there = 2 * ((x + j) & 3) + ((c + (j >> 2)) & 1)
    for t in range(tables):
        used = [jnp.where(l < lens[t : t + 1, :], owner[t, l : l + 1, :], -1) for l in range(bag)]
        vals = [value[t, l : l + 1, :] for l in range(bag)]
        for k in range(out.shape[0]):
            ids = there + k * 8
            total = jnp.zeros((8, bags), I32)
            for l in range(bag):
                total = total + jnp.where(used[l] == ids, vals[l], 0)
            out[k, 8 * t : 8 * t + 8, :] = total


STEPS = (1, 2, 2, 2, 1)


def prep_kernel(order, pos, codes, *refs):
    ranks, sides, code_all, rank_all = refs[:5], refs[5:10], refs[10], refs[11]
    bags = code_all.shape[1]
    for s in range(8):
        code_all[16 * s : 16 * s + 16, :] = codes[lax.rem(pos[0] + 8 - order[s], 8)]
    earlier = (
        lax.broadcasted_iota(I32, (bags, bags), 0) < lax.broadcasted_iota(I32, (bags, bags), 1)
    )
    earlier = jnp.where(earlier, 1.0, 0.0).astype(BF16)
    present = code_all[...] > 0
    rank = jnp.dot(jnp.where(present, 1.0, 0.0).astype(BF16), earlier, preferred_element_type=F32)
    rank_all[...] = jnp.where(present, rank, 255.0)
    first = 0
    for step, count in enumerate(STEPS):

        def unit(i, carry):
            at = pl.ds(pl.multiple_of((first + i) * 8, 8), 8)
            code = code_all[at, :]
            ranks[step][i] = rank_all[at, :]
            row = lax.shift_right_logical(code, 11)
            fields = [
                lax.shift_right_logical(row, 2).astype(F32),
                (code & 2047).astype(F32) * (1.0 / 512.0),
                (row & 3).astype(F32),
                jnp.zeros((128 - 24, bags), F32),
            ]
            sides[step][i] = jnp.concatenate(fields, axis=0).T.astype(BF16)
            return carry

        lax.fori_loop(0, 2 * count, unit, 0)
        first += 2 * count


def pick_kernel(count, ranks, sides, *refs):
    blocks, refs = refs[:2], refs[2:]
    outs, bag_all, picks, rhs = refs[:12], refs[12], refs[13], refs[14]
    bags = bag_all.shape[2]
    if count == 1:
        for t in range(2):
            bag_all[0, t] = blocks[t][...]
    else:
        for s in range(2):
            for t in range(2):
                bag_all[s, t] = blocks[s][t * bags : (t + 1) * bags, :]
    place = lax.broadcasted_iota(I32, (MOST, bags), 0).astype(F32).astype(BF16)

    def source(s, carry):
        for t in range(2):
            rhs[t, :, :128] = bag_all[s, t]
            rhs[t, :, 128:] = sides[2 * s + t]
            rank = ranks[2 * s + t].astype(BF16)
            for o in range(8):
                line = jnp.broadcast_to(rank[o : o + 1, :], (MOST, bags))
                picks[t, o * MOST : (o + 1) * MOST, :] = jnp.where(
                    line == place, jnp.ones((), BF16), jnp.zeros((), BF16)
                )
        for t in range(2):
            for o in range(0, 8, 2):
                got2 = jnp.dot(
                    picks[t, o * MOST : (o + 2) * MOST, :], rhs[t], preferred_element_type=F32
                )
                for i in range(2):
                    q = o + i
                    got = got2[i * MOST : (i + 1) * MOST]
                    rows, low, meta = outs[3 * (2 * t + q // 4) : 3 * (2 * t + q // 4) + 3]
                    k = q % 4
                    rows[s, k] = got[:, :128].astype(BF16)
                    low[s, k] = jnp.broadcast_to(
                        got[:, 128 + 16 + q : 128 + 17 + q], (MOST, 128)
                    ).astype(BF16)
                    side = got[:, 128:].T
                    meta[s, k : k + 1, :] = side[q : q + 1]
                    meta[s, 4 + k : 5 + k, :] = side[8 + q : 9 + q]
        return carry

    lax.fori_loop(0, count, source, 0)


def spread_one(k, steps, onto, both):
    ids = lax.broadcasted_iota(I32, (256, MOST), 0).astype(F32).astype(BF16)
    s = 0
    for rows, low, meta in steps:
        for i in range(rows.shape[0]):
            at = slice(s * MOST, (s + 1) * MOST)
            high = jnp.broadcast_to(meta[i, pl.ds(k, 1), :].astype(BF16), (256, MOST))
            wt = jnp.broadcast_to(meta[i, pl.ds(k + 4, 1), :].astype(BF16), (256, MOST))
            onto[:, at] = jnp.where(high == ids, wt, jnp.zeros((), BF16))
            vec, bits = rows[i, k], low[i, k]
            for l in range(4):
                both[at, l * 128 : (l + 1) * 128] = jnp.where(
                    bits == jnp.full((), l, BF16), vec, jnp.zeros((), BF16)
                )
            s += 1
    return jnp.dot(onto[...], both[...], preferred_element_type=F32)


def send_kernel(*refs):
    steps = [refs[3 * i : 3 * i + 3] for i in range(5)]
    out, onto, both = refs[15:]

    def one(k, carry):
        out[k] = spread_one(k, steps, onto, both).astype(BF16)
        return carry

    lax.fori_loop(0, 4, one, 0)


def keep_kernel(other, *refs):
    steps = [refs[3 * i : 3 * i + 3] for i in range(5)]
    outs, onto, both, total = refs[15:19], refs[19], refs[20], refs[21]

    def one(k, carry):
        total[k] = spread_one(k, steps, onto, both) + other[k].astype(F32)
        return carry

    lax.fori_loop(0, 4, one, 0)
    for k in range(4):
        outs[k][...] = total[k].astype(outs[k].dtype)


def grad_kernel(pos, pooled, delta, keep, send, half):
    x, c = pos[1], pos[2]

    def piece(i, carry):
        at = pl.ds(pl.multiple_of(i * 512, 512), 512)
        half[...] = lax.dot_general(
            pooled[:, at], delta[...], (((0,), (0,)), ((), ())), preferred_element_type=F32
        )
        for j in range(4):
            kz = i * 4 + j
            for k in range(4):
                row = j * 128 + lax.rem(x + k, 4) * 32
                keep[k, kz] = half[pl.ds(pl.multiple_of(row + c * 16, 16), 16), :]
                send[k, kz] = half[pl.ds(pl.multiple_of(row + (1 - c) * 16, 16), 16), :]
        return carry

    lax.fori_loop(0, 2, piece, 0)


def finish_kernel(pos, total, blocks, out):
    z = pos[0]
    acc = total[z]
    for k in range(1, 8):
        acc = acc + blocks[lax.rem(z + k, 8)].astype(F32)
    out[...] = acc


def leave_kernel(slots_s, goal_s, accum_s, weight, slot_out, weight_out, accum_out):
    slot_out[...] = jnp.full_like(slot_out, -1.0)
    weight_out[...] = jnp.zeros_like(weight_out)
    accum_out[...] = jnp.zeros_like(accum_out)

    def leave(i, carry):
        for j in range(4):
            slot, goal = slots_s[4 * i + j], goal_s[4 * i + j]
            at = pl.ds(goal, 1)
            slot_out[at, :] = jnp.full((1, 128), slot, I32).astype(F32)
            weight_out[at, :] = weight[pl.ds(slot, 1), :]
            accum_out[at, :] = jnp.full((1, 128), accum_s[slot], F32)
        return carry

    lax.fori_loop(0, slots_s.shape[0] // 4, leave, 0)


def square():
    return lax.broadcasted_iota(I32, (128, 128), 0) == lax.broadcasted_iota(I32, (128, 128), 1)


def evict_kernel(slot_map, slot_in, weight, accum, *refs):
    parts, rhs, held, pick = refs[:8], refs[8], refs[9:13], refs[13]
    for t in range(2):
        own = parts[4 * t][...]
        for k in range(1, 4):
            own = own + parts[4 * t + k][...].astype(F32)
        high = own.astype(BF16)
        low = (own - high.astype(F32)).astype(BF16)
        for l in range(4):
            at = (4 * t + l) * 256
            rhs[at : at + 256, :128] = high[:, l * 128 : (l + 1) * 128]
            rhs[at : at + 256, 128:] = low[:, l * 128 : (l + 1) * 128]
    eye = square()

    def block(k, carry):
        at = pl.ds(pl.multiple_of(k * 128, 128), 128)
        slots = slot_in[at, :]
        for i in range(16):
            lane = slice(i * 128, (i + 1) * 128)
            pick[:, lane] = jnp.where(slots == slot_map[:, lane], 1.0, 0.0).astype(BF16)
        both = jnp.dot(pick[...], rhs[...], preferred_element_type=F32)
        g = both[:, :128] + both[:, 128:]
        acc = accum[at, :] + jnp.sum(g * g, axis=1, keepdims=True) * (1.0 / 128.0)
        row = weight[at, :] - LEARN_RATE * g / (jnp.sqrt(acc) + EPSILON)
        line = jnp.sum(jnp.where(eye, acc, 0.0), axis=0, keepdims=True)
        for i in range(4):

            @pl.when(k == i)
            def _():
                held[i][:128, :] = row
                held[i][128:, :] = jnp.broadcast_to(line, (HELD - 128, 128))

        return carry

    lax.fori_loop(0, 4, block, 0)


def update_kernel(slot_map, rhs, weight, accum, new_weight, new_accum):
    eye = square()
    step = 256
    ids = lax.broadcasted_iota(I32, (step, 2048), 0).astype(F32).astype(BF16)
    slot_row = slot_map[...]

    def chunk(i, carry):
        at = pl.multiple_of(i * step, step)
        near = slot_row - at.astype(F32)
        near = jnp.where((near >= 0.0) & (near < step), near, 2.0 * step).astype(BF16)
        pick = jnp.where(
            jnp.broadcast_to(near, (step, 2048)) == ids, jnp.ones((), BF16), jnp.zeros((), BF16)
        )
        both = jnp.dot(pick, rhs[...], preferred_element_type=F32)
        grad = both[:, :128] + both[:, 128:]
        for j in range(step // 128):
            g = grad[j * 128 : (j + 1) * 128]
            b = i * (step // 128) + j
            kept = jnp.sum(jnp.where(eye, accum[pl.ds(b, 1), :], 0.0), axis=1, keepdims=True)
            acc = kept + jnp.sum(g * g, axis=1, keepdims=True) * (1.0 / 128.0)
            here = pl.ds(pl.multiple_of(at + j * 128, 128), 128)
            new_accum[pl.ds(b, 1), :] = jnp.sum(jnp.where(eye, acc, 0.0), axis=0, keepdims=True)
            new_weight[here, :] = weight[here, :] - LEARN_RATE * g / (jnp.sqrt(acc) + EPSILON)
        return carry

    lax.fori_loop(0, 2048 // step, chunk, 0)


def arrive_kernel(pos, b0, b1, b2, b3, rows, accum):
    h = pos[3]
    for k, ref in enumerate((b0, b1, b2, b3)):
        at = lax.rem(h + 4 - k, 4)
        rows[at] = ref[:128, :]
        accum[pl.ds(at, 1), :] = ref[128:129, :]


def together(*groups):
    flat = [a for g in groups for a in g]
    flat = lax.optimization_barrier(flat)
    out = []
    for g in groups:
        out.append(flat[: len(g)])
        flat = flat[len(g) :]
    return out


def on_device(
    pooled,
    w_up,
    grad_out,
    owners,
    rows,
    lookup_weight,
    lens,
    slot_map,
    cache_weight,
    cache_accum,
    evict_slots,
    evict_dest,
    evict_count,
):
    shape = jax.ShapeDtypeStruct
    bags = pooled.shape[0]
    z, x, c, h = (lax.axis_index(a) for a in (Z, X, C, H))
    pos = jnp.stack([z, x, c, h]).astype(I32)

    delta, *parts = call(
        top_kernel,
        [SMEM, VMEM, VMEM, VMEM],
        [shape((bags, 1024), BF16), shape((2 * bags, 128), F32)] + [shape((2 * bags, 128), BF16)] * 3,
        [pltpu.VMEM((4, bags, 256), F32)],
        2 << 30,
        6 << 20,
        "top",
    )(pos, pooled, w_up, grad_out)
    got = [shifted(parts[k], H, k) for k in (1, 2, 3)]

    value = rows * 2048 + (lookup_weight.astype(F32) * 512.0).astype(I32)
    (codes,) = call(
        code_kernel, [SMEM, VMEM, VMEM, VMEM], [shape((8, 16, bags), I32)], [], 1 << 22, 1 << 20, "codes"
    )(pos, jnp.swapaxes(owners, 1, 2), jnp.swapaxes(value, 1, 2), lens)
    codes = lax.all_to_all(codes, Z, split_axis=0, concat_axis=0, tiled=True)

    got, (codes,) = together(got, (codes,))
    own = parts[0] + got[0].astype(F32) + got[1].astype(F32) + got[2].astype(F32)
    own = own.astype(BF16)
    order = (0, 1, 7, 2, 6, 3, 5, 4)
    units = [2 * n for n in STEPS]
    prep = call(
        functools.partial(prep_kernel, order),
        [SMEM, VMEM],
        [shape((n, 8, bags), F32) for n in units] + [shape((n, bags, 128), BF16) for n in units],
        [pltpu.VMEM((128, bags), I32), pltpu.VMEM((128, bags), F32)],
        1 << 26,
        3 << 20,
        "prep",
    )(pos, codes)

    def pick(step, blocks):
        count = STEPS[step]
        outs = [
            shape((count, 4, MOST, 128), BF16),
            shape((count, 4, MOST, 128), BF16),
            shape((count, 8, 128), F32),
        ] * 4
        return call(
            functools.partial(pick_kernel, count),
            [VMEM] * 4,
            outs,
            [
                pltpu.VMEM((count, 2, bags, 128), BF16),
                pltpu.VMEM((2, 8 * MOST, bags), BF16),
                pltpu.VMEM((2, bags, 256), BF16),
            ],
            1 << 30,
            4 << 20,
            f"pick{step}",
        )(prep[step], prep[5 + step], *blocks)

    up, down = shifted(own, Z, 1), shifted(own, Z, -1)
    (delta,), (own,) = together((delta,), (own,))
    grad, there = call(
        grad_kernel,
        [SMEM, VMEM, VMEM],
        [shape((4, 8, 16, 1024), F32)] * 2,
        [pltpu.VMEM((512, 1024), F32)],
        1 << 30,
        6 << 20,
        "grad",
    )(pos, pooled, delta)
    near = (up, down)
    (up, down), (grad, there) = together((up, down), (grad, there))
    there = shifted(there, C, 1)
    up, down = shifted(up, Z, 1), shifted(down, Z, -1)
    picked = [pick(0, (own[:bags], own[bags:]))]
    mid = (up, down)
    (up, down), near, *picked = together((up, down), near, *picked)
    up, down = shifted(up, Z, 1), shifted(down, Z, -1)
    grad_x = grad + there
    total, blocks = grad_x[0], [grad_x[k].astype(BF16) for k in (1, 2, 3)]
    near, (total,), blocks = together(near, (total,), blocks)
    got_x = [shifted(blocks[k - 1], X, k) for k in (1, 2, 3)]
    picked.append(pick(1, near))
    far = (up, down)
    (up, down), mid, picked[1] = together((up, down), mid, picked[1])
    last = (shifted(up[:bags], Z, 1), shifted(down[bags:], Z, -1))
    picked.append(pick(2, mid))
    far, picked[2] = together(far, picked[2])
    picked.append(pick(3, far))
    last, got_x, picked[3] = together(last, got_x, picked[3])
    picked.append(pick(4, last))

    work = [pltpu.VMEM((256, 8 * MOST), BF16), pltpu.VMEM((8 * MOST, 512), BF16)]
    half = lambda t, side: [a for p in picked for a in p[3 * (2 * t + side) : 3 * (2 * t + side) + 3]]
    others = []
    for t in range(2):
        if others:
            others, picked[4] = together(others, picked[4])
        (out,) = call(
            send_kernel, [VMEM] * 15, [shape((4, 256, 512), BF16)], work, 4 << 30, 5 << 20, f"send{t}"
        )(*half(t, 1))
        others.append(out)
    others = [shifted(out, C, 1) for out in others]
    arrived = []
    for t in range(2):
        outs = call(
            keep_kernel,
            [VMEM] * 16,
            [shape((256, 512), F32)] + [shape((256, 512), BF16)] * 3,
            work + [pltpu.VMEM((4, 256, 512), F32)],
            4 << 30,
            5 << 20,
            f"keep{t}",
        )(others[t], *half(t, 0))
        if t == 0:
            outs, (others[1],) = together(outs, (others[1],))
        arrived += [outs[0]] + [shifted(outs[k], X, k) for k in (1, 2, 3)]

    for block in got_x:
        total = total + block.astype(F32)
    first, total, slot_map, evict_slots, evict_dest = lax.optimization_barrier(
        (arrived[5], total, slot_map, evict_slots, evict_dest)
    )
    arrived[5] = first
    blocks = lax.all_to_all(total.astype(BF16), Z, split_axis=0, concat_axis=0, tiled=True)
    (grad_up,) = call(
        finish_kernel,
        [SMEM, VMEM, VMEM],
        [shape((16, 1024), F32)],
        [],
        1 << 10,
        1 << 18,
        "finish",
    )(pos, total, blocks)

    list_len = evict_slots.shape[-1]
    departure = evict_dest[0, 0]
    list_ids = jnp.arange(list_len, dtype=I32)
    live = list_ids < evict_count[0, 0]
    picks = ((departure[:, None] == jnp.arange(4, dtype=I32)) & live[:, None]).astype(BF16)
    before = (list_ids[:, None] > list_ids[None, :]).astype(BF16)
    counted = jnp.dot(before, picks, preferred_element_type=F32)
    placed = jnp.sum(counted * picks.astype(F32), axis=-1).astype(I32)
    goal = jnp.where(live, lax.rem(departure + 4 - h, 4) * 128 + placed, 512)
    slot_rows = jnp.swapaxes(slot_map.reshape(2, 256, 4), 1, 2).reshape(1, 2048).astype(F32)
    slot_rows, goal = lax.optimization_barrier((slot_rows, goal))
    leaving = call(
        leave_kernel,
        [SMEM] * 3 + [VMEM],
        [shape((520, 128), F32)] * 3,
        [],
        1 << 10,
        1 << 20,
        "leave",
    )(evict_slots.reshape(-1), goal, cache_accum.reshape(-1), cache_weight[0, 0])
    arrived, leaving = together(arrived, leaving)
    rhs, *held = call(
        evict_kernel,
        [VMEM] * 12,
        [shape((2048, 256), BF16)] + [shape((HELD, 128), F32)] * 4,
        [pltpu.VMEM((128, 2048), BF16)],
        1 << 29,
        4 << 20,
        "evict",
    )(slot_rows, *leaving, *arrived)
    moved = [shifted(held[k], H, k) for k in (1, 2, 3)]
    new_weight, new_accum = call(
        update_kernel,
        [VMEM] * 4,
        [shape((2048, 128), F32), shape((16, 128), F32)],
        [],
        2 << 30,
        4 << 20,
        "update",
    )(slot_rows, rhs, cache_weight[0, 0], cache_accum.reshape(16, 128))
    held = [held[0]] + moved
    held_rows, held_accum = call(
        arrive_kernel,
        [SMEM] + [VMEM] * 4,
        [shape((4, 128, 128), F32), shape((4, 128), F32)],
        [],
        1 << 10,
        1 << 19,
        "arrive",
    )(pos, *held)
    return (
        grad_up,
        new_weight[None, None],
        new_accum.reshape(1, 1, 2048),
        held_rows[None, None],
        held_accum[None, None],
    )


def solution(mesh):
    torus = Mesh(mesh.devices.reshape(8, 4, 2, mesh.shape["hst"]), (Z, X, C, H))
    in_specs = (
        P(TBL, None),
        P(None, "hst"),
        P(TBL, "hst"),
        P("hst", TBL, None),
        P("hst", TBL, None),
        P("hst", TBL, None),
        P("hst", TBL),
        P(TBL, "hst", None),
        P(TBL, "hst", None, None),
        P(TBL, "hst", None),
        P(TBL, "hst", None),
        P(TBL, "hst", None),
        P(TBL, "hst"),
    )
    out_specs = (
        P(TBL, "hst"),
        P(TBL, "hst", None, None),
        P(TBL, "hst", None),
        P(TBL, "hst", None, None, None),
        P(TBL, "hst", None, None),
    )
    return jax.shard_map(
        on_device, mesh=torus, in_specs=in_specs, out_specs=out_specs, check_vma=False
    )
```

```python
import functools

import jax
import jax.numpy as jnp
from jax import lax
from jax.experimental import pallas as pl
from jax.experimental.pallas import tpu as pltpu
from jax.sharding import Mesh
from jax.sharding import PartitionSpec as P

TBL = ("tbl_0", "tbl_1", "tbl_2")
Z, X, C, H = "tbl_0", "tbl_1", "tbl_2", "hst"

LEARN_RATE = 0.05
EPSILON = 1e-08
F32 = jnp.float32
BF16 = jnp.bfloat16
I32 = jnp.int32
VMEM = pl.BlockSpec(memory_space=pltpu.VMEM)
SMEM = pl.BlockSpec(memory_space=pltpu.SMEM)
MOST = 128
HELD = 136


def shifted(x, axis, step):
    size = lax.axis_size(axis)
    return lax.ppermute(x, axis, [(i, (i + step) % size) for i in range(size)])


def call(body, ins, outs, scratch, flops, moved, name):
    return pl.pallas_call(
        body,
        in_specs=ins,
        out_specs=[VMEM] * len(outs),
        out_shape=outs,
        scratch_shapes=scratch,
        compiler_params=pltpu.CompilerParams(vmem_limit_bytes=20 << 20),
        cost_estimate=pl.CostEstimate(flops=flops, bytes_accessed=moved, transcendentals=0),
        name=name,
    )


def top_kernel(pos, pooled, w_up, grad_out, delta, own, one, two, three, feature):
    width = 256

    def column(i, carry):
        at = pl.ds(pl.multiple_of(i * width, width), width)
        preact = jnp.dot(pooled[...], w_up[:, at], preferred_element_type=F32)
        s = jax.nn.sigmoid(preact)
        delta[:, at] = (grad_out[:, at].astype(F32) * s * (1.0 + preact * (1.0 - s))).astype(BF16)
        return carry

    lax.fori_loop(0, 4, column, 0)
    h = pos[3]

    def part(k, carry):
        row = pl.multiple_of(lax.rem(h + k, 4) * width, width)
        feature[k] = lax.dot_general(
            delta[...],
            w_up[pl.ds(row, width), :],
            (((1,), (1,)), ((), ())),
            preferred_element_type=F32,
        )
        return carry

    lax.fori_loop(0, 4, part, 0)
    bags = delta.shape[0]
    for k, ref in enumerate((own, one, two, three)):
        for t in range(2):
            ref[t * bags : (t + 1) * bags, :] = feature[k, :, t * 128 : (t + 1) * 128].astype(ref.dtype)


def field_kernel(owner, row, weight, lens, out, earlier_out):
    tables, bag, bags = owner.shape
    for t in range(tables):
        slot = lax.broadcasted_iota(I32, (bag, bags), 0)
        used = jnp.where(slot < lens[t : t + 1, :], owner[t], 64)
        fields = [used, lax.shift_right_logical(row[t], 2), row[t] & 3]
        fields = [f.astype(F32) for f in fields] + [weight[t].astype(F32)]
        fields = jnp.concatenate(fields, axis=0).astype(BF16)
        for q in range(4):
            out[t, q * 32 : (q + 1) * 32, :] = fields[:, q * 128 : (q + 1) * 128]
    shape = earlier_out.shape
    earlier = lax.broadcasted_iota(I32, shape, 0) < lax.broadcasted_iota(I32, shape, 1)
    earlier_out[...] = jnp.where(earlier, 1.0, 0.0).astype(BF16)


def own_kernel(own, one, two, three, fields, out):
    bags, lines = own.shape[0] // 2, fields.shape[1]
    for t in range(2):
        at = slice(t * bags, (t + 1) * bags)
        total = own[at, :] + one[at, :].astype(F32) + two[at, :].astype(F32) + three[at, :].astype(F32)
        first = t * (bags + lines)
        out[first : first + bags, :] = total.astype(BF16)
        out[first + bags : first + bags + lines, :] = fields[t]


STEPS = (1, 2, 2, 2, 1)


def pick_kernel(count, pos, earlier, *refs):
    blocks = 2 if count == 2 or len(refs) == 19 else 1
    msgs, refs = refs[:blocks], refs[blocks:]
    outs, (bag_all, dense, ranks, picks, rhs) = refs[:12], refs[12:]
    bags = bag_all.shape[2]
    units = 2 * count
    lines = 128
    z, x, c = pos[0], pos[1], pos[2]
    j = lax.broadcasted_iota(I32, (8, bags), 0)
    ids = (z * 8 + 2 * ((x + j) & 3) + ((c + (j >> 2)) & 1)).astype(F32)
    for s in range(count):
        for t in range(2):
            if count == 2:
                ref, first = msgs[s], t * (bags + lines)
            elif blocks == 2:
                ref, first = msgs[t], 0
            else:
                ref, first = msgs[0], t * (bags + lines)
            bag_all[s, t] = ref[first : first + bags, :]
            first += bags
            fields = jnp.concatenate(
                [ref[first + q * 32 : first + (q + 1) * 32, :].astype(F32) for q in range(4)], axis=1
            )
            high = jnp.zeros((8, bags), F32)
            low, weight = high, high
            for l in range(8):
                mine = fields[l : l + 1] == ids
                high = high + jnp.where(mine, fields[8 + l : 9 + l], 0.0)
                low = low + jnp.where(mine, fields[16 + l : 17 + l], 0.0)
                weight = weight + jnp.where(mine, fields[24 + l : 25 + l], 0.0)
            u = 2 * s + t
            dense[u, 0:8] = high
            dense[u, 8:16] = weight
            dense[u, 16:24] = low
    present = jnp.concatenate([dense[u, 8:16] for u in range(units)], axis=0) > 0.0
    rank = jnp.dot(
        jnp.where(present, 1.0, 0.0).astype(BF16), earlier[...], preferred_element_type=F32
    )
    rank = jnp.where(present, rank, 255.0)
    for u in range(units):
        ranks[u] = rank[8 * u : 8 * u + 8]
    place = lax.broadcasted_iota(I32, (MOST, bags), 0).astype(F32).astype(BF16)

    def source(s, carry):
        for t in range(2):
            u = 2 * s + t
            rhs[t, :, :128] = bag_all[s, t]
            moved = jnp.concatenate([dense[u], jnp.zeros((128 - 24, bags), F32)], axis=0)
            rhs[t, :, 128:] = moved.T.astype(BF16)
            rank = ranks[u].astype(BF16)
            for o in range(8):
                line = jnp.broadcast_to(rank[o : o + 1, :], (MOST, bags))
                picks[t, o * MOST : (o + 1) * MOST, :] = jnp.where(
                    line == place, jnp.ones((), BF16), jnp.zeros((), BF16)
                )
        for t in range(2):
            for o in range(0, 8, 2):
                got2 = jnp.dot(
                    picks[t, o * MOST : (o + 2) * MOST, :], rhs[t], preferred_element_type=F32
                )
                for i in range(2):
                    q = o + i
                    got = got2[i * MOST : (i + 1) * MOST]
                    rows, low, meta = outs[3 * (2 * t + q // 4) : 3 * (2 * t + q // 4) + 3]
                    k = q % 4
                    rows[s, k] = got[:, :128].astype(BF16)
                    low[s, k] = jnp.broadcast_to(
                        got[:, 128 + 16 + q : 128 + 17 + q], (MOST, 128)
                    ).astype(BF16)
                    side = got[:, 128:].T
                    meta[s, k : k + 1, :] = side[q : q + 1]
                    meta[s, 4 + k : 5 + k, :] = side[8 + q : 9 + q]
        return carry

    lax.fori_loop(0, count, source, 0)


def spread_one(k, steps, onto, both):
    ids = lax.broadcasted_iota(I32, (256, MOST), 0).astype(F32).astype(BF16)
    s = 0
    for rows, low, meta in steps:
        for i in range(rows.shape[0]):
            at = slice(s * MOST, (s + 1) * MOST)
            high = jnp.broadcast_to(meta[i, pl.ds(k, 1), :].astype(BF16), (256, MOST))
            wt = jnp.broadcast_to(meta[i, pl.ds(k + 4, 1), :].astype(BF16), (256, MOST))
            onto[:, at] = jnp.where(high == ids, wt, jnp.zeros((), BF16))
            vec, bits = rows[i, k], low[i, k]
            for l in range(4):
                both[at, l * 128 : (l + 1) * 128] = jnp.where(
                    bits == jnp.full((), l, BF16), vec, jnp.zeros((), BF16)
                )
            s += 1
    return jnp.dot(onto[...], both[...], preferred_element_type=F32)


def send_kernel(*refs):
    steps = [refs[3 * i : 3 * i + 3] for i in range(5)]
    out, onto, both = refs[15:]

    def one(k, carry):
        out[k] = spread_one(k, steps, onto, both).astype(BF16)
        return carry

    lax.fori_loop(0, 4, one, 0)


def keep_kernel(other0, other1, *refs):
    outs, onto, both, total = refs[30:34], refs[34], refs[35], refs[36]
    for t, other in enumerate((other0, other1)):
        steps = [refs[15 * t + 3 * i : 15 * t + 3 * i + 3] for i in range(5)]

        def one(k, carry):
            total[k] = spread_one(k, steps, onto, both) + other[k].astype(F32)
            return carry

        lax.fori_loop(0, 4, one, 0)
        for k in range(4):
            outs[k][t * 256 : (t + 1) * 256, :] = total[k].astype(outs[k].dtype)


def grad_kernel(pos, pooled, delta, keep, send, half):
    x, c = pos[1], pos[2]

    def piece(i, carry):
        at = pl.ds(pl.multiple_of(i * 512, 512), 512)
        half[...] = lax.dot_general(
            pooled[:, at], delta[...], (((0,), (0,)), ((), ())), preferred_element_type=F32
        )
        for j in range(4):
            kz = i * 4 + j
            for k in range(4):
                row = j * 128 + lax.rem(x + k, 4) * 32
                keep[k, kz] = half[pl.ds(pl.multiple_of(row + c * 16, 16), 16), :]
                send[k, kz] = half[pl.ds(pl.multiple_of(row + (1 - c) * 16, 16), 16), :]
        return carry

    lax.fori_loop(0, 2, piece, 0)


def finish_kernel(pos, total, blocks, out):
    z = pos[0]
    acc = total[z]
    for k in range(1, 8):
        acc = acc + blocks[lax.rem(z + k, 8)].astype(F32)
    out[...] = acc


def leave_kernel(slots_s, goal_s, accum_s, weight, slot_out, weight_out, accum_out):
    slot_out[...] = jnp.full_like(slot_out, -1.0)
    weight_out[...] = jnp.zeros_like(weight_out)
    accum_out[...] = jnp.zeros_like(accum_out)

    def leave(i, carry):
        for j in range(4):
            slot, goal = slots_s[4 * i + j], goal_s[4 * i + j]
            at = pl.ds(goal, 1)
            slot_out[at, :] = jnp.full((1, 128), slot, I32).astype(F32)
            weight_out[at, :] = weight[pl.ds(slot, 1), :]
            accum_out[at, :] = jnp.full((1, 128), accum_s[slot], F32)
        return carry

    lax.fori_loop(0, slots_s.shape[0] // 4, leave, 0)


def square():
    return lax.broadcasted_iota(I32, (128, 128), 0) == lax.broadcasted_iota(I32, (128, 128), 1)


def evict_kernel(slot_map, slot_in, weight, accum, *refs):
    parts, rhs, held, pick, sums = refs[:4], refs[4], refs[5:9], refs[9], refs[10]
    for t in range(2):
        at = slice(t * 256, (t + 1) * 256)
        own = parts[0][at, :]
        for k in range(1, 4):
            own = own + parts[k][at, :].astype(F32)
        high = own.astype(BF16)
        low = (own - high.astype(F32)).astype(BF16)
        for l in range(4):
            at = (4 * t + l) * 256
            rhs[at : at + 256, :128] = high[:, l * 128 : (l + 1) * 128]
            rhs[at : at + 256, 128:] = low[:, l * 128 : (l + 1) * 128]
    eye = square()
    for i in range(16):
        lane = slice(i * 128, (i + 1) * 128)
        pick[:, lane] = jnp.where(slot_in[:512, :] == slot_map[:, lane], 1.0, 0.0).astype(BF16)
    sums[...] = jnp.dot(pick[...], rhs[...], preferred_element_type=F32)
    for i in range(4):
        at = slice(i * 128, (i + 1) * 128)
        g = sums[at, :128] + sums[at, 128:]
        acc = accum[at, :] + jnp.sum(g * g, axis=1, keepdims=True) * (1.0 / 128.0)
        held[i][:128, :] = weight[at, :] - LEARN_RATE * g / (jnp.sqrt(acc) + EPSILON)
        line = jnp.sum(jnp.where(eye, acc, 0.0), axis=0, keepdims=True)
        held[i][128:, :] = jnp.broadcast_to(line, (HELD - 128, 128))


def update_kernel(slot_map, rhs, weight, accum, new_weight, new_accum, pick, sums):
    eye = square()
    step, part = 512, 256
    ids = lax.broadcasted_iota(I32, (part, 2048), 0).astype(F32).astype(BF16)
    slot_row = slot_map[...]

    def chunk(i, carry):
        at = pl.multiple_of(i * step, step)
        for j in range(step // part):
            near = slot_row - (at + j * part).astype(F32)
            near = jnp.where((near >= 0.0) & (near < part), near, 2.0 * part).astype(BF16)
            pick[j * part : (j + 1) * part, :] = jnp.where(
                jnp.broadcast_to(near, (part, 2048)) == ids, jnp.ones((), BF16), jnp.zeros((), BF16)
            )
        sums[...] = jnp.dot(pick[...], rhs[...], preferred_element_type=F32)
        for j in range(step // 128):
            part_at = slice(j * 128, (j + 1) * 128)
            g = sums[part_at, :128] + sums[part_at, 128:]
            b = i * (step // 128) + j
            kept = jnp.sum(jnp.where(eye, accum[pl.ds(b, 1), :], 0.0), axis=1, keepdims=True)
            acc = kept + jnp.sum(g * g, axis=1, keepdims=True) * (1.0 / 128.0)
            here = pl.ds(pl.multiple_of(at + j * 128, 128), 128)
            new_accum[pl.ds(b, 1), :] = jnp.sum(jnp.where(eye, acc, 0.0), axis=0, keepdims=True)
            new_weight[here, :] = weight[here, :] - LEARN_RATE * g / (jnp.sqrt(acc) + EPSILON)
        return carry

    lax.fori_loop(0, 2048 // step, chunk, 0)


def arrive_kernel(pos, b0, b1, b2, b3, rows, accum):
    h = pos[3]
    for k, ref in enumerate((b0, b1, b2, b3)):
        at = lax.rem(h + 4 - k, 4)
        rows[at] = ref[:128, :]
        accum[pl.ds(at, 1), :] = ref[128:129, :]


def together(*groups):
    flat = [a for g in groups for a in g]
    flat = lax.optimization_barrier(flat)
    out = []
    for g in groups:
        out.append(flat[: len(g)])
        flat = flat[len(g) :]
    return out


def on_device(
    pooled,
    w_up,
    grad_out,
    owners,
    rows,
    lookup_weight,
    lens,
    slot_map,
    cache_weight,
    cache_accum,
    evict_slots,
    evict_dest,
    evict_count,
):
    shape = jax.ShapeDtypeStruct
    bags = pooled.shape[0]
    z, x, c, h = (lax.axis_index(a) for a in (Z, X, C, H))
    pos = jnp.stack([z, x, c, h]).astype(I32)

    delta, *parts = call(
        top_kernel,
        [SMEM, VMEM, VMEM, VMEM],
        [shape((bags, 1024), BF16), shape((2 * bags, 128), F32)] + [shape((2 * bags, 128), BF16)] * 3,
        [pltpu.VMEM((4, bags, 256), F32)],
        2 << 30,
        6 << 20,
        "top",
    )(pos, pooled, w_up, grad_out)
    got = [shifted(parts[k], H, k) for k in (1, 2, 3)]

    (delta,), (owners, rows, lookup_weight, lens) = together(
        (delta,), (owners, rows, lookup_weight, lens)
    )
    fields, earlier = call(
        field_kernel,
        [VMEM] * 4,
        [shape((2, 128, 128), BF16), shape((bags, bags), BF16)],
        [],
        1 << 20,
        1 << 20,
        "fields",
    )(*[jnp.swapaxes(a, 1, 2) for a in (owners, rows, lookup_weight)], lens)
    (own,) = call(
        own_kernel, [VMEM] * 5, [shape((2 * (bags + 128), 128), BF16)], [], 1 << 20, 2 << 20, "own"
    )(parts[0], *got, fields)

    def pick(step, blocks):
        count = STEPS[step]
        outs = [
            shape((count, 4, MOST, 128), BF16),
            shape((count, 4, MOST, 128), BF16),
            shape((count, 8, 128), F32),
        ] * 4
        return call(
            functools.partial(pick_kernel, count),
            [SMEM, VMEM] + [VMEM] * len(blocks),
            outs,
            [
                pltpu.VMEM((count, 2, bags, 128), BF16),
                pltpu.VMEM((2 * count, 24, bags), F32),
                pltpu.VMEM((2 * count, 8, bags), F32),
                pltpu.VMEM((2, 8 * MOST, bags), BF16),
                pltpu.VMEM((2, bags, 256), BF16),
            ],
            1 << 30,
            4 << 20,
            f"pick{step}",
        )(pos, earlier, *blocks)

    up, down = shifted(own, Z, 1), shifted(own, Z, -1)
    (delta,), (own,) = together((delta,), (own,))
    grad, there = call(
        grad_kernel,
        [SMEM, VMEM, VMEM],
        [shape((4, 8, 16, 1024), F32)] * 2,
        [pltpu.VMEM((512, 1024), F32)],
        1 << 30,
        6 << 20,
        "grad",
    )(pos, pooled, delta)
    near = (up, down)
    (up, down), (grad, there) = together((up, down), (grad, there))
    there = shifted(there, C, 1)
    up, down = shifted(up, Z, 1), shifted(down, Z, -1)
    picked = [pick(0, (own,))]
    mid = (up, down)
    (up, down), near, *picked = together((up, down), near, *picked)
    up, down = shifted(up, Z, 1), shifted(down, Z, -1)
    grad_x = grad + there
    total, blocks = grad_x[0], [grad_x[k].astype(BF16) for k in (1, 2, 3)]
    near, (total,), blocks = together(near, (total,), blocks)
    got_x = [shifted(blocks[k - 1], X, k) for k in (1, 2, 3)]
    picked.append(pick(1, near))
    far = (up, down)
    (up, down), mid, picked[1] = together((up, down), mid, picked[1])
    part = bags + 128
    last = (shifted(up[:part], Z, 1), shifted(down[part:], Z, -1))
    picked.append(pick(2, mid))
    far, picked[2] = together(far, picked[2])
    picked.append(pick(3, far))
    last, got_x, picked[3] = together(last, got_x, picked[3])
    picked.append(pick(4, last))

    work = [pltpu.VMEM((256, 8 * MOST), BF16), pltpu.VMEM((8 * MOST, 512), BF16)]
    half = lambda t, side: [a for p in picked for a in p[3 * (2 * t + side) : 3 * (2 * t + side) + 3]]
    others = []
    for t in range(2):
        if others:
            others, picked[4] = together(others, picked[4])
        (out,) = call(
            send_kernel, [VMEM] * 15, [shape((4, 256, 512), BF16)], work, 4 << 30, 5 << 20, f"send{t}"
        )(*half(t, 1))
        others.append(out)
    others = [shifted(out, C, 1) for out in others]
    outs = call(
        keep_kernel,
        [VMEM] * 32,
        [shape((512, 512), F32)] + [shape((512, 512), BF16)] * 3,
        work + [pltpu.VMEM((4, 256, 512), F32)],
        8 << 30,
        10 << 20,
        "keep",
    )(*others, *half(0, 0), *half(1, 0))
    arrived = [outs[0]] + [shifted(outs[k], X, k) for k in (1, 2, 3)]

    for block in got_x:
        total = total + block.astype(F32)
    first, total, slot_map, evict_slots, evict_dest = lax.optimization_barrier(
        (arrived[0], total, slot_map, evict_slots, evict_dest)
    )
    arrived[0] = first
    blocks = lax.all_to_all(total.astype(BF16), Z, split_axis=0, concat_axis=0, tiled=True)
    (grad_up,) = call(
        finish_kernel,
        [SMEM, VMEM, VMEM],
        [shape((16, 1024), F32)],
        [],
        1 << 10,
        1 << 18,
        "finish",
    )(pos, total, blocks)

    list_len = evict_slots.shape[-1]
    departure = evict_dest[0, 0]
    list_ids = jnp.arange(list_len, dtype=I32)
    live = list_ids < evict_count[0, 0]
    picks = ((departure[:, None] == jnp.arange(4, dtype=I32)) & live[:, None]).astype(BF16)
    before = (list_ids[:, None] > list_ids[None, :]).astype(BF16)
    counted = jnp.dot(before, picks, preferred_element_type=F32)
    placed = jnp.sum(counted * picks.astype(F32), axis=-1).astype(I32)
    goal = jnp.where(live, lax.rem(departure + 4 - h, 4) * 128 + placed, 512)
    slot_rows = jnp.swapaxes(slot_map.reshape(2, 256, 4), 1, 2).reshape(1, 2048).astype(F32)
    slot_rows, goal = lax.optimization_barrier((slot_rows, goal))
    leaving = call(
        leave_kernel,
        [SMEM] * 3 + [VMEM],
        [shape((520, 128), F32)] * 3,
        [],
        1 << 10,
        1 << 20,
        "leave",
    )(evict_slots.reshape(-1), goal, cache_accum.reshape(-1), cache_weight[0, 0])
    arrived, leaving = together(arrived, leaving)
    rhs, *held = call(
        evict_kernel,
        [VMEM] * 8,
        [shape((2048, 256), BF16)] + [shape((HELD, 128), F32)] * 4,
        [pltpu.VMEM((512, 2048), BF16), pltpu.VMEM((512, 256), F32)],
        1 << 29,
        4 << 20,
        "evict",
    )(slot_rows, *leaving, *arrived)
    moved = [shifted(held[k], H, k) for k in (1, 2, 3)]
    new_weight, new_accum = call(
        update_kernel,
        [VMEM] * 4,
        [shape((2048, 128), F32), shape((16, 128), F32)],
        [pltpu.VMEM((512, 2048), BF16), pltpu.VMEM((512, 256), F32)],
        2 << 30,
        4 << 20,
        "update",
    )(slot_rows, rhs, cache_weight[0, 0], cache_accum.reshape(16, 128))
    held = [held[0]] + moved
    held_rows, held_accum = call(
        arrive_kernel,
        [SMEM] + [VMEM] * 4,
        [shape((4, 128, 128), F32), shape((4, 128), F32)],
        [],
        1 << 10,
        1 << 19,
        "arrive",
    )(pos, *held)
    return (
        grad_up,
        new_weight[None, None],
        new_accum.reshape(1, 1, 2048),
        held_rows[None, None],
        held_accum[None, None],
    )


def solution(mesh):
    torus = Mesh(mesh.devices.reshape(8, 4, 2, mesh.shape["hst"]), (Z, X, C, H))
    in_specs = (
        P(TBL, None),
        P(None, "hst"),
        P(TBL, "hst"),
        P("hst", TBL, None),
        P("hst", TBL, None),
        P("hst", TBL, None),
        P("hst", TBL),
        P(TBL, "hst", None),
        P(TBL, "hst", None, None),
        P(TBL, "hst", None),
        P(TBL, "hst", None),
        P(TBL, "hst", None),
        P(TBL, "hst"),
    )
    out_specs = (
        P(TBL, "hst"),
        P(TBL, "hst", None, None),
        P(TBL, "hst", None),
        P(TBL, "hst", None, None, None),
        P(TBL, "hst", None, None),
    )
    return jax.shard_map(
        on_device, mesh=torus, in_specs=in_specs, out_specs=out_specs, check_vma=False
    )
```

```python
import functools

import jax
import jax.numpy as jnp
from jax import lax
from jax.experimental import pallas as pl
from jax.experimental.pallas import tpu as pltpu
from jax.sharding import Mesh
from jax.sharding import PartitionSpec as P

TBL = ("tbl_0", "tbl_1", "tbl_2")
Z, X, C, H = "tbl_0", "tbl_1", "tbl_2", "hst"

LEARN_RATE = 0.05
EPSILON = 1e-08
F32 = jnp.float32
BF16 = jnp.bfloat16
I32 = jnp.int32
VMEM = pl.BlockSpec(memory_space=pltpu.VMEM)
SMEM = pl.BlockSpec(memory_space=pltpu.SMEM)
MOST = 128
HELD = 136


def shifted(x, axis, step):
    size = lax.axis_size(axis)
    return lax.ppermute(x, axis, [(i, (i + step) % size) for i in range(size)])


def call(body, ins, outs, scratch, micros, name):
    return pl.pallas_call(
        body,
        in_specs=ins,
        out_specs=[VMEM] * len(outs),
        out_shape=outs,
        scratch_shapes=scratch,
        compiler_params=pltpu.CompilerParams(vmem_limit_bytes=20 << 20),
        cost_estimate=pl.CostEstimate(
            flops=1 << 20, bytes_accessed=int(micros * 3.5e6), transcendentals=0
        ),
        name=name,
    )


def top_kernel(pos, pooled, w_up, grad_out, delta, own, one, two, three, feature):
    width = 256

    def column(i, carry):
        at = pl.ds(pl.multiple_of(i * width, width), width)
        preact = jnp.dot(pooled[...], w_up[:, at], preferred_element_type=F32)
        s = jax.nn.sigmoid(preact)
        delta[:, at] = (grad_out[:, at].astype(F32) * s * (1.0 + preact * (1.0 - s))).astype(BF16)
        return carry

    lax.fori_loop(0, 4, column, 0)
    h = pos[3]

    def part(k, carry):
        row = pl.multiple_of(lax.rem(h + k, 4) * width, width)
        feature[k] = lax.dot_general(
            delta[...],
            w_up[pl.ds(row, width), :],
            (((1,), (1,)), ((), ())),
            preferred_element_type=F32,
        )
        return carry

    lax.fori_loop(0, 4, part, 0)
    bags = delta.shape[0]
    for k, ref in enumerate((own, one, two, three)):
        for t in range(2):
            ref[t * bags : (t + 1) * bags, :] = feature[k, :, t * 128 : (t + 1) * 128].astype(ref.dtype)


def field_kernel(owner, row, weight, lens, out, earlier_out):
    tables, bag, bags = owner.shape
    for t in range(tables):
        slot = lax.broadcasted_iota(I32, (bag, bags), 0)
        used = jnp.where(slot < lens[t : t + 1, :], owner[t], 64)
        fields = [used, lax.shift_right_logical(row[t], 2), row[t] & 3]
        fields = [f.astype(F32) for f in fields] + [weight[t].astype(F32)]
        fields = jnp.concatenate(fields, axis=0).astype(BF16)
        for q in range(4):
            out[t, q * 32 : (q + 1) * 32, :] = fields[:, q * 128 : (q + 1) * 128]
    shape = earlier_out.shape
    earlier = lax.broadcasted_iota(I32, shape, 0) < lax.broadcasted_iota(I32, shape, 1)
    earlier_out[...] = jnp.where(earlier, 1.0, 0.0).astype(BF16)


def own_kernel(own, one, two, three, fields, out):
    bags, lines = own.shape[0] // 2, fields.shape[1]
    for t in range(2):
        at = slice(t * bags, (t + 1) * bags)
        total = own[at, :] + one[at, :].astype(F32) + two[at, :].astype(F32) + three[at, :].astype(F32)
        first = t * (bags + lines)
        out[first : first + bags, :] = total.astype(BF16)
        out[first + bags : first + bags + lines, :] = fields[t]


STEPS = (1, 2, 2, 2, 1)


def pick_kernel(count, pos, earlier, *refs):
    msg, refs = refs[0], refs[1:]
    outs, (bag_all, dense, ranks, picks, rhs) = refs[:12], refs[12:]
    bags = bag_all.shape[2]
    units = 2 * count
    lines = 128
    z, x, c = pos[0], pos[1], pos[2]
    j = lax.broadcasted_iota(I32, (8, bags), 0)
    ids = (z * 8 + 2 * ((x + j) & 3) + ((c + (j >> 2)) & 1)).astype(F32)
    for s in range(count):
        for t in range(2):
            ref, first = (msg.at[s] if count == 2 else msg), t * (bags + lines)
            bag_all[s, t] = ref[first : first + bags, :]
            first += bags
            fields = jnp.concatenate(
                [ref[first + q * 32 : first + (q + 1) * 32, :].astype(F32) for q in range(4)], axis=1
            )
            high = jnp.zeros((8, bags), F32)
            low, weight = high, high
            for l in range(8):
                mine = fields[l : l + 1] == ids
                high = high + jnp.where(mine, fields[8 + l : 9 + l], 0.0)
                low = low + jnp.where(mine, fields[16 + l : 17 + l], 0.0)
                weight = weight + jnp.where(mine, fields[24 + l : 25 + l], 0.0)
            u = 2 * s + t
            dense[u, 0:8] = high
            dense[u, 8:16] = weight
            dense[u, 16:24] = low
    present = jnp.concatenate([dense[u, 8:16] for u in range(units)], axis=0) > 0.0
    rank = jnp.dot(
        jnp.where(present, 1.0, 0.0).astype(BF16), earlier[...], preferred_element_type=F32
    )
    rank = jnp.where(present, rank, 255.0)
    for u in range(units):
        ranks[u] = rank[8 * u : 8 * u + 8]
    place = lax.broadcasted_iota(I32, (MOST, bags), 0).astype(F32).astype(BF16)

    def source(s, carry):
        for t in range(2):
            u = 2 * s + t
            rhs[t, :, :128] = bag_all[s, t]
            moved = jnp.concatenate([dense[u], jnp.zeros((128 - 24, bags), F32)], axis=0)
            rhs[t, :, 128:] = moved.T.astype(BF16)
            rank = ranks[u].astype(BF16)
            for o in range(8):
                line = jnp.broadcast_to(rank[o : o + 1, :], (MOST, bags))
                picks[t, o * MOST : (o + 1) * MOST, :] = jnp.where(
                    line == place, jnp.ones((), BF16), jnp.zeros((), BF16)
                )
        for t in range(2):
            for o in range(0, 8, 2):
                got2 = jnp.dot(
                    picks[t, o * MOST : (o + 2) * MOST, :], rhs[t], preferred_element_type=F32
                )
                for i in range(2):
                    q = o + i
                    got = got2[i * MOST : (i + 1) * MOST]
                    rows, low, meta = outs[3 * (2 * t + q // 4) : 3 * (2 * t + q // 4) + 3]
                    k = q % 4
                    rows[s, k] = got[:, :128].astype(BF16)
                    low[s, k] = jnp.broadcast_to(
                        got[:, 128 + 16 + q : 128 + 17 + q], (MOST, 128)
                    ).astype(BF16)
                    side = got[:, 128:].T
                    meta[s, k : k + 1, :] = side[q : q + 1]
                    meta[s, 4 + k : 5 + k, :] = side[8 + q : 9 + q]
        return carry

    lax.fori_loop(0, count, source, 0)


def spread_one(k, steps, onto, both):
    ids = lax.broadcasted_iota(I32, (256, MOST), 0).astype(F32).astype(BF16)
    s = 0
    for rows, low, meta in steps:
        for i in range(rows.shape[0]):
            at = slice(s * MOST, (s + 1) * MOST)
            high = jnp.broadcast_to(meta[i, pl.ds(k, 1), :].astype(BF16), (256, MOST))
            wt = jnp.broadcast_to(meta[i, pl.ds(k + 4, 1), :].astype(BF16), (256, MOST))
            onto[:, at] = jnp.where(high == ids, wt, jnp.zeros((), BF16))
            vec, bits = rows[i, k], low[i, k]
            for l in range(4):
                both[at, l * 128 : (l + 1) * 128] = jnp.where(
                    bits == jnp.full((), l, BF16), vec, jnp.zeros((), BF16)
                )
            s += 1
    return jnp.dot(onto[...], both[...], preferred_element_type=F32)


def send_kernel(*refs):
    steps = [refs[3 * i : 3 * i + 3] for i in range(5)]
    out, onto, both = refs[15:]

    def one(k, carry):
        out[k] = spread_one(k, steps, onto, both).astype(BF16)
        return carry

    lax.fori_loop(0, 4, one, 0)


def keep_kernel(other0, other1, *refs):
    outs, mark, onto, both, total = refs[30:34], refs[34], refs[35], refs[36], refs[37]
    for t, other in enumerate((other0, other1)):
        steps = [refs[15 * t + 3 * i : 15 * t + 3 * i + 3] for i in range(5)]

        def one(k, carry):
            total[k] = spread_one(k, steps, onto, both) + other[k].astype(F32)
            return carry

        lax.fori_loop(0, 4, one, 0)
        for k in range(4):
            outs[k][t * 256 : (t + 1) * 256, :] = total[k].astype(outs[k].dtype)
    mark[...] = total[0, :8, :128]


def grad_kernel(pos, pooled, delta, keep, send, half):
    x, c = pos[1], pos[2]

    def piece(i, carry):
        at = pl.ds(pl.multiple_of(i * 512, 512), 512)
        half[...] = lax.dot_general(
            pooled[:, at], delta[...], (((0,), (0,)), ((), ())), preferred_element_type=F32
        )
        for j in range(4):
            kz = i * 4 + j
            for k in range(4):
                row = j * 128 + lax.rem(x + k, 4) * 32
                keep[k, kz] = half[pl.ds(pl.multiple_of(row + c * 16, 16), 16), :]
                send[k, kz] = half[pl.ds(pl.multiple_of(row + (1 - c) * 16, 16), 16), :]
        return carry

    lax.fori_loop(0, 2, piece, 0)


def finish_kernel(pos, total, blocks, out):
    z = pos[0]
    acc = total[z]
    for k in range(1, 8):
        acc = acc + blocks[lax.rem(z + k, 8)].astype(F32)
    out[...] = acc


def leave_kernel(slots_s, goal_s, accum_s, weight, slot_out, weight_out, accum_out):
    slot_out[...] = jnp.full_like(slot_out, -1.0)
    weight_out[...] = jnp.zeros_like(weight_out)
    accum_out[...] = jnp.zeros_like(accum_out)

    def leave(i, carry):
        for j in range(4):
            slot, goal = slots_s[4 * i + j], goal_s[4 * i + j]
            at = pl.ds(goal, 1)
            slot_out[at, :] = jnp.full((1, 128), slot, I32).astype(F32)
            weight_out[at, :] = weight[pl.ds(slot, 1), :]
            accum_out[at, :] = jnp.full((1, 128), accum_s[slot], F32)
        return carry

    lax.fori_loop(0, slots_s.shape[0] // 4, leave, 0)


def square():
    return lax.broadcasted_iota(I32, (128, 128), 0) == lax.broadcasted_iota(I32, (128, 128), 1)


def evict_kernel(slot_map, slot_in, weight, accum, *refs):
    parts, rhs, held, pick, sums = refs[:4], refs[4], refs[5:9], refs[9], refs[10]
    for t in range(2):
        at = slice(t * 256, (t + 1) * 256)
        own = parts[0][at, :]
        for k in range(1, 4):
            own = own + parts[k][at, :].astype(F32)
        high = own.astype(BF16)
        low = (own - high.astype(F32)).astype(BF16)
        for l in range(4):
            at = (4 * t + l) * 256
            rhs[at : at + 256, :128] = high[:, l * 128 : (l + 1) * 128]
            rhs[at : at + 256, 128:] = low[:, l * 128 : (l + 1) * 128]
    eye = square()
    for i in range(16):
        lane = slice(i * 128, (i + 1) * 128)
        pick[:, lane] = jnp.where(slot_in[:512, :] == slot_map[:, lane], 1.0, 0.0).astype(BF16)
    sums[...] = jnp.dot(pick[...], rhs[...], preferred_element_type=F32)
    for i in range(4):
        at = slice(i * 128, (i + 1) * 128)
        g = sums[at, :128] + sums[at, 128:]
        acc = accum[at, :] + jnp.sum(g * g, axis=1, keepdims=True) * (1.0 / 128.0)
        held[i][:128, :] = weight[at, :] - LEARN_RATE * g / (jnp.sqrt(acc) + EPSILON)
        line = jnp.sum(jnp.where(eye, acc, 0.0), axis=0, keepdims=True)
        held[i][128:, :] = jnp.broadcast_to(line, (HELD - 128, 128))


def update_kernel(slot_map, rhs, weight, accum, new_weight, new_accum, pick, sums):
    eye = square()
    step, part = 512, 256
    ids = lax.broadcasted_iota(I32, (part, 2048), 0).astype(F32).astype(BF16)
    slot_row = slot_map[...]

    def chunk(i, carry):
        at = pl.multiple_of(i * step, step)
        for j in range(step // part):
            near = slot_row - (at + j * part).astype(F32)
            near = jnp.where((near >= 0.0) & (near < part), near, 2.0 * part).astype(BF16)
            pick[j * part : (j + 1) * part, :] = jnp.where(
                jnp.broadcast_to(near, (part, 2048)) == ids, jnp.ones((), BF16), jnp.zeros((), BF16)
            )
        sums[...] = jnp.dot(pick[...], rhs[...], preferred_element_type=F32)
        for j in range(step // 128):
            part_at = slice(j * 128, (j + 1) * 128)
            g = sums[part_at, :128] + sums[part_at, 128:]
            b = i * (step // 128) + j
            kept = jnp.sum(jnp.where(eye, accum[pl.ds(b, 1), :], 0.0), axis=1, keepdims=True)
            acc = kept + jnp.sum(g * g, axis=1, keepdims=True) * (1.0 / 128.0)
            here = pl.ds(pl.multiple_of(at + j * 128, 128), 128)
            new_accum[pl.ds(b, 1), :] = jnp.sum(jnp.where(eye, acc, 0.0), axis=0, keepdims=True)
            new_weight[here, :] = weight[here, :] - LEARN_RATE * g / (jnp.sqrt(acc) + EPSILON)
        return carry

    lax.fori_loop(0, 2048 // step, chunk, 0)


def arrive_kernel(pos, b0, b1, b2, b3, rows, accum):
    h = pos[3]
    for k, ref in enumerate((b0, b1, b2, b3)):
        at = lax.rem(h + 4 - k, 4)
        rows[at] = ref[:128, :]
        accum[pl.ds(at, 1), :] = ref[128:129, :]


def together(*groups):
    flat = [a for g in groups for a in g]
    flat = lax.optimization_barrier(flat)
    out = []
    for g in groups:
        out.append(flat[: len(g)])
        flat = flat[len(g) :]
    return out


def on_device(
    pooled,
    w_up,
    grad_out,
    owners,
    rows,
    lookup_weight,
    lens,
    slot_map,
    cache_weight,
    cache_accum,
    evict_slots,
    evict_dest,
    evict_count,
):
    shape = jax.ShapeDtypeStruct
    bags = pooled.shape[0]
    z, x, c, h = (lax.axis_index(a) for a in (Z, X, C, H))
    pos = jnp.stack([z, x, c, h]).astype(I32)

    delta, *parts = call(
        top_kernel,
        [SMEM, VMEM, VMEM, VMEM],
        [shape((bags, 1024), BF16), shape((2 * bags, 128), F32)] + [shape((2 * bags, 128), BF16)] * 3,
        [pltpu.VMEM((4, bags, 256), F32)],
        4.5,
        "top",
    )(pos, pooled, w_up, grad_out)
    got = [shifted(parts[k], H, k) for k in (1, 2, 3)]

    (delta,), (owners, rows, lookup_weight, lens) = together(
        (delta,), (owners, rows, lookup_weight, lens)
    )
    fields, earlier = call(
        field_kernel,
        [VMEM] * 4,
        [shape((2, 128, 128), BF16), shape((bags, bags), BF16)],
        [],
        1.0,
        "fields",
    )(*[jnp.swapaxes(a, 1, 2) for a in (owners, rows, lookup_weight)], lens)
    (own,) = call(
        own_kernel, [VMEM] * 5, [shape((2 * (bags + 128), 128), BF16)], [], 0.5, "own"
    )(parts[0], *got, fields)

    def pick(step, block):
        count = STEPS[step]
        outs = [
            shape((count, 4, MOST, 128), BF16),
            shape((count, 4, MOST, 128), BF16),
            shape((count, 8, 128), F32),
        ] * 4
        return call(
            functools.partial(pick_kernel, count),
            [SMEM, VMEM, VMEM],
            outs,
            [
                pltpu.VMEM((count, 2, bags, 128), BF16),
                pltpu.VMEM((2 * count, 24, bags), F32),
                pltpu.VMEM((2 * count, 8, bags), F32),
                pltpu.VMEM((2, 8 * MOST, bags), BF16),
                pltpu.VMEM((2, bags, 256), BF16),
            ],
            2.8,
            f"pick{step}",
        )(pos, earlier, block)

    ways = [(2 * i, 2 * ((i + 1) % 8)) for i in range(8)]
    ways += [(2 * i + 1, 2 * ((i + 7) % 8) + 1) for i in range(8)]

    def passed(message):
        return lax.ppermute(message, (Z, C), ways)

    near = passed(jnp.stack([own, shifted(own, C, 1)]))
    (delta,), (own,) = together((delta,), (own,))
    grad, there = call(
        grad_kernel,
        [SMEM, VMEM, VMEM],
        [shape((4, 8, 16, 1024), F32)] * 2,
        [pltpu.VMEM((512, 1024), F32)],
        2.3,
        "grad",
    )(pos, pooled, delta)
    picked = [pick(0, own)]
    (near,), (grad, there), picked[0] = together((near,), (grad, there), picked[0])
    there = shifted(there, C, 1)
    mid = passed(near)
    picked.append(pick(1, near))
    (mid,), picked[1] = together((mid,), picked[1])
    far = passed(mid)
    (there,), (mid,) = together((there,), (mid,))
    grad_x = grad + there
    total, blocks = grad_x[0], [grad_x[k].astype(BF16) for k in (1, 2, 3)]
    got_x = [shifted(blocks[k - 1], X, k) for k in (1, 2, 3)]
    last = passed(far[0])
    (mid,), (total,), (far,) = together((mid,), (total,), (far,))
    picked.append(pick(2, mid))
    picked.append(pick(3, far))
    (last,), got_x, picked[3] = together((last,), got_x, picked[3])
    picked.append(pick(4, last))

    work = [pltpu.VMEM((256, 8 * MOST), BF16), pltpu.VMEM((8 * MOST, 512), BF16)]
    half = lambda t, side: [a for p in picked for a in p[3 * (2 * t + side) : 3 * (2 * t + side) + 3]]
    others = []
    for t in range(2):
        if others:
            others, picked[4] = together(others, picked[4])
        (out,) = call(
            send_kernel, [VMEM] * 15, [shape((4, 256, 512), BF16)], work, 2.5, f"send{t}"
        )(*half(t, 1))
        others.append(out)
    others = [shifted(out, C, 1) for out in others]
    outs = call(
        keep_kernel,
        [VMEM] * 32,
        [shape((512, 512), F32)] + [shape((512, 512), BF16)] * 3 + [shape((8, 128), F32)],
        work + [pltpu.VMEM((4, 256, 512), F32)],
        6.3,
        "keep",
    )(*others, *half(0, 0), *half(1, 0))
    arrived = [outs[0]] + [shifted(outs[k], X, k) for k in (1, 2, 3)]

    for block in got_x:
        total = total + block.astype(F32)
    _, total, slot_map, evict_slots, evict_dest = lax.optimization_barrier(
        (outs[4], total, slot_map, evict_slots, evict_dest)
    )
    blocks = lax.all_to_all(total.astype(BF16), Z, split_axis=0, concat_axis=0, tiled=True)
    (grad_up,) = call(
        finish_kernel,
        [SMEM, VMEM, VMEM],
        [shape((16, 1024), F32)],
        [],
        1.2,
        "finish",
    )(pos, total, blocks)

    list_len = evict_slots.shape[-1]
    departure = evict_dest[0, 0]
    list_ids = jnp.arange(list_len, dtype=I32)
    live = list_ids < evict_count[0, 0]
    picks = ((departure[:, None] == jnp.arange(4, dtype=I32)) & live[:, None]).astype(BF16)
    before = (list_ids[:, None] > list_ids[None, :]).astype(BF16)
    counted = jnp.dot(before, picks, preferred_element_type=F32)
    placed = jnp.sum(counted * picks.astype(F32), axis=-1).astype(I32)
    goal = jnp.where(live, lax.rem(departure + 4 - h, 4) * 128 + placed, 512)
    slot_rows = jnp.swapaxes(slot_map.reshape(2, 256, 4), 1, 2).reshape(1, 2048).astype(F32)
    slot_rows, goal = lax.optimization_barrier((slot_rows, goal))
    leaving = call(
        leave_kernel,
        [SMEM] * 3 + [VMEM],
        [shape((520, 128), F32)] * 3,
        [],
        1.6,
        "leave",
    )(evict_slots.reshape(-1), goal, cache_accum.reshape(-1), cache_weight[0, 0])
    rhs, *held = call(
        evict_kernel,
        [VMEM] * 8,
        [shape((2048, 256), BF16)] + [shape((HELD, 128), F32)] * 4,
        [pltpu.VMEM((512, 2048), BF16), pltpu.VMEM((512, 256), F32)],
        2.7,
        "evict",
    )(slot_rows, *leaving, *arrived)
    moved = [shifted(held[k], H, k) for k in (1, 2, 3)]
    new_weight, new_accum = call(
        update_kernel,
        [VMEM] * 4,
        [shape((2048, 128), F32), shape((16, 128), F32)],
        [pltpu.VMEM((512, 2048), BF16), pltpu.VMEM((512, 256), F32)],
        4.3,
        "update",
    )(slot_rows, rhs, cache_weight[0, 0], cache_accum.reshape(16, 128))
    held = [held[0]] + moved
    held_rows, held_accum = call(
        arrive_kernel,
        [SMEM] + [VMEM] * 4,
        [shape((4, 128, 128), F32), shape((4, 128), F32)],
        [],
        1.2,
        "arrive",
    )(pos, *held)
    return (
        grad_up,
        new_weight[None, None],
        new_accum.reshape(1, 1, 2048),
        held_rows[None, None],
        held_accum[None, None],
    )


def solution(mesh):
    torus = Mesh(mesh.devices.reshape(8, 4, 2, mesh.shape["hst"]), (Z, X, C, H))
    in_specs = (
        P(TBL, None),
        P(None, "hst"),
        P(TBL, "hst"),
        P("hst", TBL, None),
        P("hst", TBL, None),
        P("hst", TBL, None),
        P("hst", TBL),
        P(TBL, "hst", None),
        P(TBL, "hst", None, None),
        P(TBL, "hst", None),
        P(TBL, "hst", None),
        P(TBL, "hst", None),
        P(TBL, "hst"),
    )
    out_specs = (
        P(TBL, "hst"),
        P(TBL, "hst", None, None),
        P(TBL, "hst", None),
        P(TBL, "hst", None, None, None),
        P(TBL, "hst", None, None),
    )
    return jax.shard_map(
        on_device, mesh=torus, in_specs=in_specs, out_specs=out_specs, check_vma=False
    )
```

```python
import functools

import jax
import jax.numpy as jnp
from jax import lax
from jax.experimental import pallas as pl
from jax.experimental.pallas import tpu as pltpu
from jax.sharding import Mesh
from jax.sharding import PartitionSpec as P

TBL = ("tbl_0", "tbl_1", "tbl_2")
Z, X, C, H = "tbl_0", "tbl_1", "tbl_2", "hst"

LEARN_RATE = 0.05
EPSILON = 1e-08
F32 = jnp.float32
BF16 = jnp.bfloat16
I32 = jnp.int32
VMEM = pl.BlockSpec(memory_space=pltpu.VMEM)
SMEM = pl.BlockSpec(memory_space=pltpu.SMEM)
MOST = 128
HELD = 136


def shifted(x, axis, step):
    size = lax.axis_size(axis)
    return lax.ppermute(x, axis, [(i, (i + step) % size) for i in range(size)])


def call(body, ins, outs, scratch, flops, moved, name, limit=20):
    return pl.pallas_call(
        body,
        in_specs=ins,
        out_specs=[VMEM] * len(outs),
        out_shape=outs,
        scratch_shapes=scratch,
        compiler_params=pltpu.CompilerParams(vmem_limit_bytes=limit << 20),
        cost_estimate=pl.CostEstimate(flops=flops, bytes_accessed=moved, transcendentals=0),
        name=name,
    )


def top_kernel(pos, pooled, w_up, grad_out, delta, own, one, two, three, feature):
    width = 256

    def column(i, carry):
        at = pl.ds(pl.multiple_of(i * width, width), width)
        preact = jnp.dot(pooled[...], w_up[:, at], preferred_element_type=F32)
        s = jax.nn.sigmoid(preact)
        delta[:, at] = (grad_out[:, at].astype(F32) * s * (1.0 + preact * (1.0 - s))).astype(BF16)
        return carry

    lax.fori_loop(0, 4, column, 0)
    h = pos[3]

    def part(k, carry):
        row = pl.multiple_of(lax.rem(h + k, 4) * width, width)
        feature[k] = lax.dot_general(
            delta[...],
            w_up[pl.ds(row, width), :],
            (((1,), (1,)), ((), ())),
            preferred_element_type=F32,
        )
        return carry

    lax.fori_loop(0, 4, part, 0)
    bags = delta.shape[0]
    for k, ref in enumerate((own, one, two, three)):
        for t in range(2):
            ref[t * bags : (t + 1) * bags, :] = feature[k, :, t * 128 : (t + 1) * 128].astype(ref.dtype)


def field_kernel(owner, row, weight, lens, out, earlier_out):
    tables, bag, bags = owner.shape
    for t in range(tables):
        slot = lax.broadcasted_iota(I32, (bag, bags), 0)
        used = jnp.where(slot < lens[t : t + 1, :], owner[t], 64)
        fields = [used, lax.shift_right_logical(row[t], 2), row[t] & 3]
        fields = [f.astype(F32) for f in fields] + [weight[t].astype(F32)]
        fields = jnp.concatenate(fields, axis=0).astype(BF16)
        for q in range(4):
            out[t, q * 32 : (q + 1) * 32, :] = fields[:, q * 128 : (q + 1) * 128]
    shape = earlier_out.shape
    earlier = lax.broadcasted_iota(I32, shape, 0) < lax.broadcasted_iota(I32, shape, 1)
    earlier_out[...] = jnp.where(earlier, 1.0, 0.0).astype(BF16)


def own_kernel(own, one, two, three, fields, out):
    bags, lines = own.shape[0] // 2, fields.shape[1]
    for t in range(2):
        at = slice(t * bags, (t + 1) * bags)
        total = own[at, :] + one[at, :].astype(F32) + two[at, :].astype(F32) + three[at, :].astype(F32)
        first = t * (bags + lines)
        out[first : first + bags, :] = total.astype(BF16)
        out[first + bags : first + bags + lines, :] = fields[t]


STEPS = (1, 2, 2, 2, 1)


def pick_kernel(count, pos, earlier, *refs):
    blocks = 2 if count == 2 or len(refs) == 19 else 1
    msgs, refs = refs[:blocks], refs[blocks:]
    outs, (bag_all, dense, ranks, picks, rhs) = refs[:12], refs[12:]
    bags = bag_all.shape[2]
    units = 2 * count
    lines = 128
    z, x, c = pos[0], pos[1], pos[2]
    j = lax.broadcasted_iota(I32, (8, bags), 0)
    ids = (z * 8 + 2 * ((x + j) & 3) + ((c + (j >> 2)) & 1)).astype(F32)
    for s in range(count):
        for t in range(2):
            if count == 2:
                ref, first = msgs[s], t * (bags + lines)
            elif blocks == 2:
                ref, first = msgs[t], 0
            else:
                ref, first = msgs[0], t * (bags + lines)
            bag_all[s, t] = ref[first : first + bags, :]
            first += bags
            fields = jnp.concatenate(
                [ref[first + q * 32 : first + (q + 1) * 32, :].astype(F32) for q in range(4)], axis=1
            )
            high = jnp.zeros((8, bags), F32)
            low, weight = high, high
            for l in range(8):
                mine = fields[l : l + 1] == ids
                high = high + jnp.where(mine, fields[8 + l : 9 + l], 0.0)
                low = low + jnp.where(mine, fields[16 + l : 17 + l], 0.0)
                weight = weight + jnp.where(mine, fields[24 + l : 25 + l], 0.0)
            u = 2 * s + t
            dense[u, 0:8] = high
            dense[u, 8:16] = weight
            dense[u, 16:24] = low
    present = jnp.concatenate([dense[u, 8:16] for u in range(units)], axis=0) > 0.0
    rank = jnp.dot(
        jnp.where(present, 1.0, 0.0).astype(BF16), earlier[...], preferred_element_type=F32
    )
    rank = jnp.where(present, rank, 255.0)
    for u in range(units):
        ranks[u] = rank[8 * u : 8 * u + 8]
    place = lax.broadcasted_iota(I32, (MOST, bags), 0).astype(F32).astype(BF16)

    def source(s, carry):
        for t in range(2):
            u = 2 * s + t
            rhs[t, :, :128] = bag_all[s, t]
            moved = jnp.concatenate([dense[u], jnp.zeros((128 - 24, bags), F32)], axis=0)
            rhs[t, :, 128:] = moved.T.astype(BF16)
            rank = ranks[u].astype(BF16)
            for o in range(8):
                line = jnp.broadcast_to(rank[o : o + 1, :], (MOST, bags))
                picks[t, o * MOST : (o + 1) * MOST, :] = jnp.where(
                    line == place, jnp.ones((), BF16), jnp.zeros((), BF16)
                )
        for t in range(2):
            for o in range(0, 8, 2):
                got2 = jnp.dot(
                    picks[t, o * MOST : (o + 2) * MOST, :], rhs[t], preferred_element_type=F32
                )
                for i in range(2):
                    q = o + i
                    got = got2[i * MOST : (i + 1) * MOST]
                    rows, low, meta = outs[3 * (2 * t + q // 4) : 3 * (2 * t + q // 4) + 3]
                    k = q % 4
                    rows[s, k] = got[:, :128].astype(BF16)
                    low[s, k] = jnp.broadcast_to(
                        got[:, 128 + 16 + q : 128 + 17 + q], (MOST, 128)
                    ).astype(BF16)
                    side = got[:, 128:].T
                    meta[s, k : k + 1, :] = side[q : q + 1]
                    meta[s, 4 + k : 5 + k, :] = side[8 + q : 9 + q]
        return carry

    lax.fori_loop(0, count, source, 0)


def spread_one(k, steps, onto, both):
    ids = lax.broadcasted_iota(I32, (256, MOST), 0).astype(F32).astype(BF16)
    s = 0
    for rows, low, meta in steps:
        for i in range(rows.shape[0]):
            at = slice(s * MOST, (s + 1) * MOST)
            high = jnp.broadcast_to(meta[i, pl.ds(k, 1), :].astype(BF16), (256, MOST))
            wt = jnp.broadcast_to(meta[i, pl.ds(k + 4, 1), :].astype(BF16), (256, MOST))
            onto[:, at] = jnp.where(high == ids, wt, jnp.zeros((), BF16))
            vec, bits = rows[i, k], low[i, k]
            for l in range(4):
                both[at, l * 128 : (l + 1) * 128] = jnp.where(
                    bits == jnp.full((), l, BF16), vec, jnp.zeros((), BF16)
                )
            s += 1
    return jnp.dot(onto[...], both[...], preferred_element_type=F32)


def send_kernel(*refs):
    steps = [refs[3 * i : 3 * i + 3] for i in range(5)]
    out, onto, both = refs[15:]

    def one(k, carry):
        out[k] = spread_one(k, steps, onto, both).astype(BF16)
        return carry

    lax.fori_loop(0, 4, one, 0)


def keep_kernel(other0, other1, *refs):
    outs, onto, both, total = refs[30:34], refs[34], refs[35], refs[36]
    for t, other in enumerate((other0, other1)):
        steps = [refs[15 * t + 3 * i : 15 * t + 3 * i + 3] for i in range(5)]

        def one(k, carry):
            total[k] = spread_one(k, steps, onto, both) + other[k].astype(F32)
            return carry

        lax.fori_loop(0, 4, one, 0)
        for k in range(4):
            outs[k][t * 256 : (t + 1) * 256, :] = total[k].astype(outs[k].dtype)


def grad_kernel(pos, pooled, delta, keep, send, half):
    x, c = pos[1], pos[2]

    def piece(i, carry):
        at = pl.ds(pl.multiple_of(i * 512, 512), 512)
        half[...] = lax.dot_general(
            pooled[:, at], delta[...], (((0,), (0,)), ((), ())), preferred_element_type=F32
        )
        for j in range(4):
            kz = i * 4 + j
            for k in range(4):
                row = j * 128 + lax.rem(x + k, 4) * 32
                keep[k, kz] = half[pl.ds(pl.multiple_of(row + c * 16, 16), 16), :]
                send[k, kz] = half[pl.ds(pl.multiple_of(row + (1 - c) * 16, 16), 16), :]
        return carry

    lax.fori_loop(0, 2, piece, 0)


def finish_kernel(pos, total, blocks, out):
    z = pos[0]
    acc = total[z]
    for k in range(1, 8):
        acc = acc + blocks[lax.rem(z + k, 8)].astype(F32)
    out[...] = acc


def leave_kernel(slots_s, goal_s, accum_s, weight, out):
    slot_out, weight_out, accum_out = (out.at[i] for i in range(3))
    slot_out[...] = jnp.full(slot_out.shape, -1.0, F32)
    weight_out[...] = jnp.zeros(slot_out.shape, F32)
    accum_out[...] = jnp.zeros(slot_out.shape, F32)

    def leave(i, carry):
        for j in range(4):
            slot, goal = slots_s[4 * i + j], goal_s[4 * i + j]
            at = pl.ds(goal, 1)
            slot_out[at, :] = jnp.full((1, 128), slot, I32).astype(F32)
            weight_out[at, :] = weight[pl.ds(slot, 1), :]
            accum_out[at, :] = jnp.full((1, 128), accum_s[slot], F32)
        return carry

    lax.fori_loop(0, slots_s.shape[0] // 4, leave, 0)


def square():
    return lax.broadcasted_iota(I32, (128, 128), 0) == lax.broadcasted_iota(I32, (128, 128), 1)


def evict_kernel(slot_map, leaving, *refs):
    slot_in, weight, accum = (leaving.at[i] for i in range(3))
    parts, rhs, held, pick, sums = refs[:4], refs[4], refs[5:9], refs[9], refs[10]
    for t in range(2):
        at = slice(t * 256, (t + 1) * 256)
        own = parts[0][at, :]
        for k in range(1, 4):
            own = own + parts[k][at, :].astype(F32)
        high = own.astype(BF16)
        low = (own - high.astype(F32)).astype(BF16)
        for l in range(4):
            at = (4 * t + l) * 256
            rhs[at : at + 256, :128] = high[:, l * 128 : (l + 1) * 128]
            rhs[at : at + 256, 128:] = low[:, l * 128 : (l + 1) * 128]
    eye = square()
    for i in range(16):
        lane = slice(i * 128, (i + 1) * 128)
        pick[:, lane] = jnp.where(slot_in[:512, :] == slot_map[:, lane], 1.0, 0.0).astype(BF16)
    sums[...] = jnp.dot(pick[...], rhs[...], preferred_element_type=F32)
    for i in range(4):
        at = slice(i * 128, (i + 1) * 128)
        g = sums[at, :128] + sums[at, 128:]
        acc = accum[at, :] + jnp.sum(g * g, axis=1, keepdims=True) * (1.0 / 128.0)
        held[i][:128, :] = weight[at, :] - LEARN_RATE * g / (jnp.sqrt(acc) + EPSILON)
        line = jnp.sum(jnp.where(eye, acc, 0.0), axis=0, keepdims=True)
        held[i][128:, :] = jnp.broadcast_to(line, (HELD - 128, 128))


def update_kernel(slot_map, rhs, weight, accum, new_weight, new_accum, pick, sums):
    eye = square()
    step, part = 512, 256
    ids = lax.broadcasted_iota(I32, (part, 2048), 0).astype(F32).astype(BF16)
    slot_row = slot_map[...]

    def chunk(i, carry):
        at = pl.multiple_of(i * step, step)
        for j in range(step // part):
            near = slot_row - (at + j * part).astype(F32)
            near = jnp.where((near >= 0.0) & (near < part), near, 2.0 * part).astype(BF16)
            pick[j * part : (j + 1) * part, :] = jnp.where(
                jnp.broadcast_to(near, (part, 2048)) == ids, jnp.ones((), BF16), jnp.zeros((), BF16)
            )
        sums[...] = jnp.dot(pick[...], rhs[...], preferred_element_type=F32)
        for j in range(step // 128):
            part_at = slice(j * 128, (j + 1) * 128)
            g = sums[part_at, :128] + sums[part_at, 128:]
            b = i * (step // 128) + j
            kept = jnp.sum(jnp.where(eye, accum[pl.ds(b, 1), :], 0.0), axis=1, keepdims=True)
            acc = kept + jnp.sum(g * g, axis=1, keepdims=True) * (1.0 / 128.0)
            here = pl.ds(pl.multiple_of(at + j * 128, 128), 128)
            new_accum[pl.ds(b, 1), :] = jnp.sum(jnp.where(eye, acc, 0.0), axis=0, keepdims=True)
            new_weight[here, :] = weight[here, :] - LEARN_RATE * g / (jnp.sqrt(acc) + EPSILON)
        return carry

    lax.fori_loop(0, 2048 // step, chunk, 0)


def arrive_kernel(pos, b0, b1, b2, b3, rows, accum):
    h = pos[3]
    for k, ref in enumerate((b0, b1, b2, b3)):
        at = lax.rem(h + 4 - k, 4)
        rows[at] = ref[:128, :]
        accum[pl.ds(at, 1), :] = ref[128:129, :]


def together(*groups):
    flat = [a for g in groups for a in g]
    flat = lax.optimization_barrier(flat)
    out = []
    for g in groups:
        out.append(flat[: len(g)])
        flat = flat[len(g) :]
    return out


def on_device(
    pooled,
    w_up,
    grad_out,
    owners,
    rows,
    lookup_weight,
    lens,
    slot_map,
    cache_weight,
    cache_accum,
    evict_slots,
    evict_dest,
    evict_count,
):
    shape = jax.ShapeDtypeStruct
    bags = pooled.shape[0]
    z, x, c, h = (lax.axis_index(a) for a in (Z, X, C, H))
    pos = jnp.stack([z, x, c, h]).astype(I32)

    delta, *parts = call(
        top_kernel,
        [SMEM, VMEM, VMEM, VMEM],
        [shape((bags, 1024), BF16), shape((2 * bags, 128), F32)] + [shape((2 * bags, 128), BF16)] * 3,
        [pltpu.VMEM((4, bags, 256), F32)],
        2 << 30,
        6 << 20,
        "top",
        60,
    )(pos, pooled, w_up, grad_out)
    got = [shifted(parts[k], H, k) for k in (1, 2, 3)]

    (delta,), (owners, rows, lookup_weight, lens) = together(
        (delta,), (owners, rows, lookup_weight, lens)
    )
    fields, earlier = call(
        field_kernel,
        [VMEM] * 4,
        [shape((2, 128, 128), BF16), shape((bags, bags), BF16)],
        [],
        1 << 20,
        1 << 20,
        "fields",
    )(*[jnp.swapaxes(a, 1, 2) for a in (owners, rows, lookup_weight)], lens)
    (own,) = call(
        own_kernel, [VMEM] * 5, [shape((2 * (bags + 128), 128), BF16)], [], 1 << 20, 2 << 20, "own"
    )(parts[0], *got, fields)

    def pick(step, blocks):
        count = STEPS[step]
        outs = [
            shape((count, 4, MOST, 128), BF16),
            shape((count, 4, MOST, 128), BF16),
            shape((count, 8, 128), F32),
        ] * 4
        return call(
            functools.partial(pick_kernel, count),
            [SMEM, VMEM] + [VMEM] * len(blocks),
            outs,
            [
                pltpu.VMEM((count, 2, bags, 128), BF16),
                pltpu.VMEM((2 * count, 24, bags), F32),
                pltpu.VMEM((2 * count, 8, bags), F32),
                pltpu.VMEM((2, 8 * MOST, bags), BF16),
                pltpu.VMEM((2, bags, 256), BF16),
            ],
            1 << 30,
            4 << 20,
            f"pick{step}",
        )(pos, earlier, *blocks)

    up, down = shifted(own, Z, 1), shifted(own, Z, -1)
    (delta,), (own,) = together((delta,), (own,))
    grad, there = call(
        grad_kernel,
        [SMEM, VMEM, VMEM],
        [shape((4, 8, 16, 1024), F32)] * 2,
        [pltpu.VMEM((512, 1024), F32)],
        1 << 30,
        6 << 20,
        "grad",
    )(pos, pooled, delta)
    near = (up, down)
    picked = [pick(0, (own,))]
    near, (grad, there), picked[0] = together(near, (grad, there), picked[0])
    up, down = near
    there = shifted(there, C, 1)
    mid = (shifted(up, Z, 1), shifted(down, Z, -1))
    grad_x = grad + there
    total, blocks = grad_x[0], [grad_x[k].astype(BF16) for k in (1, 2, 3)]
    mid, near, (total,), blocks = together(mid, near, (total,), blocks)
    up, down = mid
    got_x = [shifted(blocks[k - 1], X, k) for k in (1, 2, 3)]
    far = (shifted(up, Z, 1), shifted(down, Z, -1))
    picked.append(pick(1, near))
    picked.append(pick(2, mid))
    far, picked[1], picked[2] = together(far, picked[1], picked[2])
    up, down = far
    part = bags + 128
    last = (shifted(up[:part], Z, 1), shifted(down[part:], Z, -1))
    picked.append(pick(3, far))
    last, got_x, picked[3] = together(last, got_x, picked[3])
    picked.append(pick(4, last))

    work = [pltpu.VMEM((256, 8 * MOST), BF16), pltpu.VMEM((8 * MOST, 512), BF16)]
    half = lambda t, side: [a for p in picked for a in p[3 * (2 * t + side) : 3 * (2 * t + side) + 3]]
    others = []
    for t in range(2):
        if others:
            others, picked[4] = together(others, picked[4])
        (out,) = call(
            send_kernel, [VMEM] * 15, [shape((4, 256, 512), BF16)], work, 4 << 30, 5 << 20, f"send{t}"
        )(*half(t, 1))
        others.append(out)
    others = [shifted(out, C, 1) for out in others]
    outs = call(
        keep_kernel,
        [VMEM] * 32,
        [shape((512, 512), F32)] + [shape((512, 512), BF16)] * 3,
        work + [pltpu.VMEM((4, 256, 512), F32)],
        8 << 30,
        10 << 20,
        "keep",
    )(*others, *half(0, 0), *half(1, 0))
    arrived = [outs[0]] + [shifted(outs[k], X, k) for k in (1, 2, 3)]

    for block in got_x:
        total = total + block.astype(F32)
    first, total, slot_map, evict_slots, evict_dest = lax.optimization_barrier(
        (arrived[0], total, slot_map, evict_slots, evict_dest)
    )
    arrived[0] = first
    blocks = lax.all_to_all(total.astype(BF16), Z, split_axis=0, concat_axis=0, tiled=True)
    (grad_up,) = call(
        finish_kernel,
        [SMEM, VMEM, VMEM],
        [shape((16, 1024), F32)],
        [],
        1 << 10,
        1 << 18,
        "finish",
    )(pos, total, blocks)

    list_len = evict_slots.shape[-1]
    departure = evict_dest[0, 0]
    list_ids = jnp.arange(list_len, dtype=I32)
    live = list_ids < evict_count[0, 0]
    picks = ((departure[:, None] == jnp.arange(4, dtype=I32)) & live[:, None]).astype(BF16)
    before = (list_ids[:, None] > list_ids[None, :]).astype(BF16)
    counted = jnp.dot(before, picks, preferred_element_type=F32)
    placed = jnp.sum(counted * picks.astype(F32), axis=-1).astype(I32)
    goal = jnp.where(live, lax.rem(departure + 4 - h, 4) * 128 + placed, 512)
    slot_rows = jnp.swapaxes(slot_map.reshape(2, 256, 4), 1, 2).reshape(1, 2048).astype(F32)
    slot_rows, goal = lax.optimization_barrier((slot_rows, goal))
    leaving = call(
        leave_kernel,
        [SMEM] * 3 + [VMEM],
        [shape((3, 520, 128), F32)],
        [],
        1 << 10,
        1 << 20,
        "leave",
    )(evict_slots.reshape(-1), goal, cache_accum.reshape(-1), cache_weight[0, 0])
    rhs, *held = call(
        evict_kernel,
        [VMEM] * 6,
        [shape((2048, 256), BF16)] + [shape((HELD, 128), F32)] * 4,
        [pltpu.VMEM((512, 2048), BF16), pltpu.VMEM((512, 256), F32)],
        1 << 29,
        4 << 20,
        "evict",
    )(slot_rows, *leaving, *arrived)
    moved = [shifted(held[k], H, k) for k in (1, 2, 3)]
    new_weight, new_accum = call(
        update_kernel,
        [VMEM] * 4,
        [shape((2048, 128), F32), shape((16, 128), F32)],
        [pltpu.VMEM((512, 2048), BF16), pltpu.VMEM((512, 256), F32)],
        2 << 30,
        4 << 20,
        "update",
    )(slot_rows, rhs, cache_weight[0, 0], cache_accum.reshape(16, 128))
    held = [held[0]] + moved
    held_rows, held_accum = call(
        arrive_kernel,
        [SMEM] + [VMEM] * 4,
        [shape((4, 128, 128), F32), shape((4, 128), F32)],
        [],
        1 << 10,
        1 << 19,
        "arrive",
    )(pos, *held)
    return (
        grad_up,
        new_weight[None, None],
        new_accum.reshape(1, 1, 2048),
        held_rows[None, None],
        held_accum[None, None],
    )


def solution(mesh):
    torus = Mesh(mesh.devices.reshape(8, 4, 2, mesh.shape["hst"]), (Z, X, C, H))
    in_specs = (
        P(TBL, None),
        P(None, "hst"),
        P(TBL, "hst"),
        P("hst", TBL, None),
        P("hst", TBL, None),
        P("hst", TBL, None),
        P("hst", TBL),
        P(TBL, "hst", None),
        P(TBL, "hst", None, None),
        P(TBL, "hst", None),
        P(TBL, "hst", None),
        P(TBL, "hst", None),
        P(TBL, "hst"),
    )
    out_specs = (
        P(TBL, "hst"),
        P(TBL, "hst", None, None),
        P(TBL, "hst", None),
        P(TBL, "hst", None, None, None),
        P(TBL, "hst", None, None),
    )
    return jax.shard_map(
        on_device, mesh=torus, in_specs=in_specs, out_specs=out_specs, check_vma=False
    )
```

```python
import functools

import jax
import jax.numpy as jnp
from jax import lax
from jax.experimental import pallas as pl
from jax.experimental.pallas import tpu as pltpu
from jax.sharding import Mesh
from jax.sharding import PartitionSpec as P

TBL = ("tbl_0", "tbl_1", "tbl_2")
Z, X, C, H = "tbl_0", "tbl_1", "tbl_2", "hst"

LEARN_RATE = 0.05
EPSILON = 1e-08
F32 = jnp.float32
BF16 = jnp.bfloat16
I32 = jnp.int32
VMEM = pl.BlockSpec(memory_space=pltpu.VMEM)
SMEM = pl.BlockSpec(memory_space=pltpu.SMEM)
MOST = 128
HELD = 136


def shifted(x, axis, step):
    size = lax.axis_size(axis)
    return lax.ppermute(x, axis, [(i, (i + step) % size) for i in range(size)])


def call(body, ins, outs, scratch, flops, moved, name, limit=20):
    return pl.pallas_call(
        body,
        in_specs=ins,
        out_specs=[VMEM] * len(outs),
        out_shape=outs,
        scratch_shapes=scratch,
        compiler_params=pltpu.CompilerParams(vmem_limit_bytes=limit << 20),
        cost_estimate=pl.CostEstimate(flops=flops, bytes_accessed=moved, transcendentals=0),
        name=name,
    )


def top_kernel(pos, pooled, w_up, grad_out, delta, own, one, two, three, feature):
    width = 256

    def column(i, carry):
        at = pl.ds(pl.multiple_of(i * width, width), width)
        preact = jnp.dot(pooled[...], w_up[:, at], preferred_element_type=F32)
        s = jax.nn.sigmoid(preact)
        delta[:, at] = (grad_out[:, at].astype(F32) * s * (1.0 + preact * (1.0 - s))).astype(BF16)
        return carry

    lax.fori_loop(0, 4, column, 0)
    h = pos[3]

    def part(k, carry):
        row = pl.multiple_of(lax.rem(h + k, 4) * width, width)
        feature[k] = lax.dot_general(
            delta[...],
            w_up[pl.ds(row, width), :],
            (((1,), (1,)), ((), ())),
            preferred_element_type=F32,
        )
        return carry

    lax.fori_loop(0, 4, part, 0)
    bags = delta.shape[0]
    for k, ref in enumerate((own, one, two, three)):
        for t in range(2):
            ref[t * bags : (t + 1) * bags, :] = feature[k, :, t * 128 : (t + 1) * 128].astype(ref.dtype)


def field_kernel(owner, row, weight, lens, out, earlier_out):
    tables, bag, bags = owner.shape
    for t in range(tables):
        slot = lax.broadcasted_iota(I32, (bag, bags), 0)
        used = jnp.where(slot < lens[t : t + 1, :], owner[t], 64)
        fields = [used, lax.shift_right_logical(row[t], 2), row[t] & 3]
        fields = [f.astype(F32) for f in fields] + [weight[t].astype(F32)]
        fields = jnp.concatenate(fields, axis=0).astype(BF16)
        for q in range(4):
            out[t, q * 32 : (q + 1) * 32, :] = fields[:, q * 128 : (q + 1) * 128]
    shape = earlier_out.shape
    earlier = lax.broadcasted_iota(I32, shape, 0) < lax.broadcasted_iota(I32, shape, 1)
    earlier_out[...] = jnp.where(earlier, 1.0, 0.0).astype(BF16)


def own_kernel(own, one, two, three, fields, out):
    bags, lines = own.shape[0] // 2, fields.shape[1]
    for t in range(2):
        at = slice(t * bags, (t + 1) * bags)
        total = own[at, :] + one[at, :].astype(F32) + two[at, :].astype(F32) + three[at, :].astype(F32)
        first = t * (bags + lines)
        out[first : first + bags, :] = total.astype(BF16)
        out[first + bags : first + bags + lines, :] = fields[t]


STEPS = (1, 2, 2, 2, 1)


def pick_kernel(count, pos, earlier, *refs):
    blocks = 2 if count == 2 or len(refs) == 19 else 1
    msgs, refs = refs[:blocks], refs[blocks:]
    outs, (bag_all, dense, ranks, picks, rhs) = refs[:12], refs[12:]
    bags = bag_all.shape[2]
    units = 2 * count
    lines = 128
    z, x, c = pos[0], pos[1], pos[2]
    j = lax.broadcasted_iota(I32, (8, bags), 0)
    ids = (z * 8 + 2 * ((x + j) & 3) + ((c + (j >> 2)) & 1)).astype(F32)
    for s in range(count):
        for t in range(2):
            if count == 2:
                ref, first = msgs[s], t * (bags + lines)
            elif blocks == 2:
                ref, first = msgs[t], 0
            else:
                ref, first = msgs[0], t * (bags + lines)
            bag_all[s, t] = ref[first : first + bags, :]
            first += bags
            fields = jnp.concatenate(
                [ref[first + q * 32 : first + (q + 1) * 32, :].astype(F32) for q in range(4)], axis=1
            )
            high = jnp.zeros((8, bags), F32)
            low, weight = high, high
            for l in range(8):
                mine = fields[l : l + 1] == ids
                high = high + jnp.where(mine, fields[8 + l : 9 + l], 0.0)
                low = low + jnp.where(mine, fields[16 + l : 17 + l], 0.0)
                weight = weight + jnp.where(mine, fields[24 + l : 25 + l], 0.0)
            u = 2 * s + t
            dense[u, 0:8] = high
            dense[u, 8:16] = weight
            dense[u, 16:24] = low
    present = jnp.concatenate([dense[u, 8:16] for u in range(units)], axis=0) > 0.0
    rank = jnp.dot(
        jnp.where(present, 1.0, 0.0).astype(BF16), earlier[...], preferred_element_type=F32
    )
    rank = jnp.where(present, rank, 255.0)
    for u in range(units):
        ranks[u] = rank[8 * u : 8 * u + 8]
    place = lax.broadcasted_iota(I32, (MOST, bags), 0).astype(F32).astype(BF16)

    def source(s, carry):
        for t in range(2):
            u = 2 * s + t
            rhs[t, :, :128] = bag_all[s, t]
            moved = jnp.concatenate([dense[u], jnp.zeros((128 - 24, bags), F32)], axis=0)
            rhs[t, :, 128:] = moved.T.astype(BF16)
            rank = ranks[u].astype(BF16)
            for o in range(8):
                line = jnp.broadcast_to(rank[o : o + 1, :], (MOST, bags))
                picks[t, o * MOST : (o + 1) * MOST, :] = jnp.where(
                    line == place, jnp.ones((), BF16), jnp.zeros((), BF16)
                )
        for t in range(2):
            for o in range(0, 8, 2):
                got2 = jnp.dot(
                    picks[t, o * MOST : (o + 2) * MOST, :], rhs[t], preferred_element_type=F32
                )
                for i in range(2):
                    q = o + i
                    got = got2[i * MOST : (i + 1) * MOST]
                    rows, low, meta = outs[3 * (2 * t + q // 4) : 3 * (2 * t + q // 4) + 3]
                    k = q % 4
                    rows[s, k] = got[:, :128].astype(BF16)
                    low[s, k] = jnp.broadcast_to(
                        got[:, 128 + 16 + q : 128 + 17 + q], (MOST, 128)
                    ).astype(BF16)
                    side = got[:, 128:].T
                    meta[s, k : k + 1, :] = side[q : q + 1]
                    meta[s, 4 + k : 5 + k, :] = side[8 + q : 9 + q]
        return carry

    lax.fori_loop(0, count, source, 0)


def spread_one(k, steps, onto, both):
    ids = lax.broadcasted_iota(I32, (256, MOST), 0).astype(F32).astype(BF16)
    s = 0
    for rows, low, meta in steps:
        for i in range(rows.shape[0]):
            at = slice(s * MOST, (s + 1) * MOST)
            high = jnp.broadcast_to(meta[i, pl.ds(k, 1), :].astype(BF16), (256, MOST))
            wt = jnp.broadcast_to(meta[i, pl.ds(k + 4, 1), :].astype(BF16), (256, MOST))
            onto[:, at] = jnp.where(high == ids, wt, jnp.zeros((), BF16))
            vec, bits = rows[i, k], low[i, k]
            for l in range(4):
                both[at, l * 128 : (l + 1) * 128] = jnp.where(
                    bits == jnp.full((), l, BF16), vec, jnp.zeros((), BF16)
                )
            s += 1
    return jnp.dot(onto[...], both[...], preferred_element_type=F32)


def send_kernel(*refs):
    steps = [refs[3 * i : 3 * i + 3] for i in range(5)]
    out, onto, both = refs[15:]

    def one(k, carry):
        out[k] = spread_one(k, steps, onto, both).astype(BF16)
        return carry

    lax.fori_loop(0, 4, one, 0)


def keep_kernel(other0, other1, *refs):
    outs, onto, both, total = refs[30:34], refs[34], refs[35], refs[36]
    for t, other in enumerate((other0, other1)):
        steps = [refs[15 * t + 3 * i : 15 * t + 3 * i + 3] for i in range(5)]

        def one(k, carry):
            total[k] = spread_one(k, steps, onto, both) + other[k].astype(F32)
            return carry

        lax.fori_loop(0, 4, one, 0)
        for k in range(4):
            outs[k][t * 256 : (t + 1) * 256, :] = total[k].astype(outs[k].dtype)


def grad_kernel(pos, pooled, delta, keep, send, half):
    x, c = pos[1], pos[2]

    def piece(i, carry):
        at = pl.ds(pl.multiple_of(i * 512, 512), 512)
        half[...] = lax.dot_general(
            pooled[:, at], delta[...], (((0,), (0,)), ((), ())), preferred_element_type=F32
        )
        for j in range(4):
            kz = i * 4 + j
            for k in range(4):
                row = j * 128 + lax.rem(x + k, 4) * 32
                keep[k, kz] = half[pl.ds(pl.multiple_of(row + c * 16, 16), 16), :]
                send[k, kz] = half[pl.ds(pl.multiple_of(row + (1 - c) * 16, 16), 16), :]
        return carry

    lax.fori_loop(0, 2, piece, 0)


def finish_kernel(pos, total, blocks, out):
    z = pos[0]
    acc = total[z]
    for k in range(1, 8):
        acc = acc + blocks[lax.rem(z + k, 8)].astype(F32)
    out[...] = acc


def leave_kernel(slots_s, goal_s, accum_s, weight, out):
    slot_out, weight_out, accum_out = (out.at[i] for i in range(3))
    slot_out[...] = jnp.full(slot_out.shape, -1.0, F32)
    weight_out[...] = jnp.zeros(slot_out.shape, F32)
    accum_out[...] = jnp.zeros(slot_out.shape, F32)

    def leave(i, carry):
        for j in range(4):
            slot, goal = slots_s[4 * i + j], goal_s[4 * i + j]
            at = pl.ds(goal, 1)
            slot_out[at, :] = jnp.full((1, 128), slot, I32).astype(F32)
            weight_out[at, :] = weight[pl.ds(slot, 1), :]
            accum_out[at, :] = jnp.full((1, 128), accum_s[slot], F32)
        return carry

    lax.fori_loop(0, slots_s.shape[0] // 4, leave, 0)


def square():
    return lax.broadcasted_iota(I32, (128, 128), 0) == lax.broadcasted_iota(I32, (128, 128), 1)


def evict_kernel(slot_map, leaving, *refs):
    slot_in, weight, accum = (leaving.at[i] for i in range(3))
    parts, rhs, held, pick, sums = refs[:4], refs[4], refs[5:9], refs[9], refs[10]
    for t in range(2):
        at = slice(t * 256, (t + 1) * 256)
        own = parts[0][at, :].astype(F32)
        for k in range(1, 4):
            own = own + parts[k][at, :].astype(F32)
        high = own.astype(BF16)
        low = (own - high.astype(F32)).astype(BF16)
        for l in range(4):
            at = (4 * t + l) * 256
            rhs[at : at + 256, :128] = high[:, l * 128 : (l + 1) * 128]
            rhs[at : at + 256, 128:] = low[:, l * 128 : (l + 1) * 128]
    eye = square()
    for i in range(16):
        lane = slice(i * 128, (i + 1) * 128)
        pick[:, lane] = jnp.where(slot_in[:512, :] == slot_map[:, lane], 1.0, 0.0).astype(BF16)
    sums[...] = jnp.dot(pick[...], rhs[...], preferred_element_type=F32)
    for i in range(4):
        at = slice(i * 128, (i + 1) * 128)
        g = sums[at, :128] + sums[at, 128:]
        acc = accum[at, :] + jnp.sum(g * g, axis=1, keepdims=True) * (1.0 / 128.0)
        held[i][:128, :] = weight[at, :] - LEARN_RATE * g / (jnp.sqrt(acc) + EPSILON)
        line = jnp.sum(jnp.where(eye, acc, 0.0), axis=0, keepdims=True)
        held[i][128:, :] = jnp.broadcast_to(line, (HELD - 128, 128))


def update_kernel(slot_map, rhs, weight, accum, new_weight, new_accum, pick, sums):
    eye = square()
    step, part = 512, 256
    ids = lax.broadcasted_iota(I32, (part, 2048), 0).astype(F32).astype(BF16)
    slot_row = slot_map[...]

    def chunk(i, carry):
        at = pl.multiple_of(i * step, step)
        for j in range(step // part):
            near = slot_row - (at + j * part).astype(F32)
            near = jnp.where((near >= 0.0) & (near < part), near, 2.0 * part).astype(BF16)
            pick[j * part : (j + 1) * part, :] = jnp.where(
                jnp.broadcast_to(near, (part, 2048)) == ids, jnp.ones((), BF16), jnp.zeros((), BF16)
            )
        sums[...] = jnp.dot(pick[...], rhs[...], preferred_element_type=F32)
        for j in range(step // 128):
            part_at = slice(j * 128, (j + 1) * 128)
            g = sums[part_at, :128] + sums[part_at, 128:]
            b = i * (step // 128) + j
            kept = jnp.sum(jnp.where(eye, accum[pl.ds(b, 1), :], 0.0), axis=1, keepdims=True)
            acc = kept + jnp.sum(g * g, axis=1, keepdims=True) * (1.0 / 128.0)
            here = pl.ds(pl.multiple_of(at + j * 128, 128), 128)
            new_accum[pl.ds(b, 1), :] = jnp.sum(jnp.where(eye, acc, 0.0), axis=0, keepdims=True)
            new_weight[here, :] = weight[here, :] - LEARN_RATE * g / (jnp.sqrt(acc) + EPSILON)
        return carry

    lax.fori_loop(0, 2048 // step, chunk, 0)


def arrive_kernel(pos, b0, b1, b2, b3, rows, accum):
    h = pos[3]
    for k, ref in enumerate((b0, b1, b2, b3)):
        at = lax.rem(h + 4 - k, 4)
        rows[at] = ref[:128, :]
        accum[pl.ds(at, 1), :] = ref[128:129, :]


def together(*groups):
    flat = [a for g in groups for a in g]
    flat = lax.optimization_barrier(flat)
    out = []
    for g in groups:
        out.append(flat[: len(g)])
        flat = flat[len(g) :]
    return out


def on_device(
    pooled,
    w_up,
    grad_out,
    owners,
    rows,
    lookup_weight,
    lens,
    slot_map,
    cache_weight,
    cache_accum,
    evict_slots,
    evict_dest,
    evict_count,
):
    shape = jax.ShapeDtypeStruct
    bags = pooled.shape[0]
    z, x, c, h = (lax.axis_index(a) for a in (Z, X, C, H))
    pos = jnp.stack([z, x, c, h]).astype(I32)

    delta, *parts = call(
        top_kernel,
        [SMEM, VMEM, VMEM, VMEM],
        [shape((bags, 1024), BF16), shape((2 * bags, 128), F32)] + [shape((2 * bags, 128), BF16)] * 3,
        [pltpu.VMEM((4, bags, 256), F32)],
        2 << 30,
        6 << 20,
        "top",
        60,
    )(pos, pooled, w_up, grad_out)
    got = [shifted(parts[k], H, k) for k in (1, 2, 3)]

    (delta,), (owners, rows, lookup_weight, lens) = together(
        (delta,), (owners, rows, lookup_weight, lens)
    )
    fields, earlier = call(
        field_kernel,
        [VMEM] * 4,
        [shape((2, 128, 128), BF16), shape((bags, bags), BF16)],
        [],
        1 << 20,
        1 << 20,
        "fields",
    )(*[jnp.swapaxes(a, 1, 2) for a in (owners, rows, lookup_weight)], lens)
    (own,) = call(
        own_kernel, [VMEM] * 5, [shape((2 * (bags + 128), 128), BF16)], [], 1 << 20, 2 << 20, "own"
    )(parts[0], *got, fields)

    def pick(step, blocks):
        count = STEPS[step]
        outs = [
            shape((count, 4, MOST, 128), BF16),
            shape((count, 4, MOST, 128), BF16),
            shape((count, 8, 128), F32),
        ] * 4
        return call(
            functools.partial(pick_kernel, count),
            [SMEM, VMEM] + [VMEM] * len(blocks),
            outs,
            [
                pltpu.VMEM((count, 2, bags, 128), BF16),
                pltpu.VMEM((2 * count, 24, bags), F32),
                pltpu.VMEM((2 * count, 8, bags), F32),
                pltpu.VMEM((2, 8 * MOST, bags), BF16),
                pltpu.VMEM((2, bags, 256), BF16),
            ],
            1 << 30,
            4 << 20,
            f"pick{step}",
        )(pos, earlier, *blocks)

    up, down = shifted(own, Z, 1), shifted(own, Z, -1)
    (delta,), (own,) = together((delta,), (own,))
    grad, there = call(
        grad_kernel,
        [SMEM, VMEM, VMEM],
        [shape((4, 8, 16, 1024), F32)] * 2,
        [pltpu.VMEM((512, 1024), F32)],
        1 << 30,
        6 << 20,
        "grad",
    )(pos, pooled, delta)
    near = (up, down)
    picked = [pick(0, (own,))]
    near, (grad, there), picked[0] = together(near, (grad, there), picked[0])
    up, down = near
    there = shifted(there, C, 1)
    mid = (shifted(up, Z, 1), shifted(down, Z, -1))
    grad_x = grad + there
    total, blocks = grad_x[0], [grad_x[k].astype(BF16) for k in (1, 2, 3)]
    mid, near, (total,), blocks = together(mid, near, (total,), blocks)
    up, down = mid
    got_x = [shifted(blocks[k - 1], X, k) for k in (1, 2, 3)]
    far = (shifted(up, Z, 1), shifted(down, Z, -1))
    picked.append(pick(1, near))
    picked.append(pick(2, mid))
    far, picked[1], picked[2] = together(far, picked[1], picked[2])
    up, down = far
    part = bags + 128
    last = (shifted(up[:part], Z, 1), shifted(down[part:], Z, -1))
    picked.append(pick(3, far))
    last, got_x, picked[3] = together(last, got_x, picked[3])
    picked.append(pick(4, last))

    work = [pltpu.VMEM((256, 8 * MOST), BF16), pltpu.VMEM((8 * MOST, 512), BF16)]
    half = lambda t, side: [a for p in picked for a in p[3 * (2 * t + side) : 3 * (2 * t + side) + 3]]
    others = []
    for t in range(2):
        if others:
            others, picked[4] = together(others, picked[4])
        (out,) = call(
            send_kernel, [VMEM] * 15, [shape((4, 256, 512), BF16)], work, 4 << 30, 5 << 20, f"send{t}"
        )(*half(t, 1))
        others.append(out)
    others = [shifted(out, C, 1) for out in others]
    outs = call(
        keep_kernel,
        [VMEM] * 32,
        [shape((512, 512), BF16)] * 4,
        work + [pltpu.VMEM((4, 256, 512), F32)],
        8 << 30,
        10 << 20,
        "keep",
    )(*others, *half(0, 0), *half(1, 0))
    arrived = [outs[0]] + [shifted(outs[k], X, k) for k in (1, 2, 3)]

    for block in got_x:
        total = total + block.astype(F32)
    first, total, slot_map, evict_slots, evict_dest = lax.optimization_barrier(
        (arrived[0], total, slot_map, evict_slots, evict_dest)
    )
    arrived[0] = first
    blocks = lax.all_to_all(total.astype(BF16), Z, split_axis=0, concat_axis=0, tiled=True)
    (grad_up,) = call(
        finish_kernel,
        [SMEM, VMEM, VMEM],
        [shape((16, 1024), F32)],
        [],
        1 << 10,
        1 << 18,
        "finish",
    )(pos, total, blocks)

    list_len = evict_slots.shape[-1]
    departure = evict_dest[0, 0]
    list_ids = jnp.arange(list_len, dtype=I32)
    live = list_ids < evict_count[0, 0]
    picks = ((departure[:, None] == jnp.arange(4, dtype=I32)) & live[:, None]).astype(BF16)
    before = (list_ids[:, None] > list_ids[None, :]).astype(BF16)
    counted = jnp.dot(before, picks, preferred_element_type=F32)
    placed = jnp.sum(counted * picks.astype(F32), axis=-1).astype(I32)
    goal = jnp.where(live, lax.rem(departure + 4 - h, 4) * 128 + placed, 512)
    slot_rows = jnp.swapaxes(slot_map.reshape(2, 256, 4), 1, 2).reshape(1, 2048).astype(F32)
    slot_rows, goal = lax.optimization_barrier((slot_rows, goal))
    leaving = call(
        leave_kernel,
        [SMEM] * 3 + [VMEM],
        [shape((3, 520, 128), F32)],
        [],
        1 << 10,
        1 << 20,
        "leave",
    )(evict_slots.reshape(-1), goal, cache_accum.reshape(-1), cache_weight[0, 0])
    rhs, *held = call(
        evict_kernel,
        [VMEM] * 6,
        [shape((2048, 256), BF16)] + [shape((HELD, 128), F32)] * 4,
        [pltpu.VMEM((512, 2048), BF16), pltpu.VMEM((512, 256), F32)],
        1 << 29,
        4 << 20,
        "evict",
    )(slot_rows, *leaving, *arrived)
    moved = [shifted(held[k], H, k) for k in (1, 2, 3)]
    new_weight, new_accum = call(
        update_kernel,
        [VMEM] * 4,
        [shape((2048, 128), F32), shape((16, 128), F32)],
        [pltpu.VMEM((512, 2048), BF16), pltpu.VMEM((512, 256), F32)],
        2 << 30,
        4 << 20,
        "update",
    )(slot_rows, rhs, cache_weight[0, 0], cache_accum.reshape(16, 128))
    held = [held[0]] + moved
    held_rows, held_accum = call(
        arrive_kernel,
        [SMEM] + [VMEM] * 4,
        [shape((4, 128, 128), F32), shape((4, 128), F32)],
        [],
        1 << 10,
        1 << 19,
        "arrive",
    )(pos, *held)
    return (
        grad_up,
        new_weight[None, None],
        new_accum.reshape(1, 1, 2048),
        held_rows[None, None],
        held_accum[None, None],
    )


def solution(mesh):
    torus = Mesh(mesh.devices.reshape(8, 4, 2, mesh.shape["hst"]), (Z, X, C, H))
    in_specs = (
        P(TBL, None),
        P(None, "hst"),
        P(TBL, "hst"),
        P("hst", TBL, None),
        P("hst", TBL, None),
        P("hst", TBL, None),
        P("hst", TBL),
        P(TBL, "hst", None),
        P(TBL, "hst", None, None),
        P(TBL, "hst", None),
        P(TBL, "hst", None),
        P(TBL, "hst", None),
        P(TBL, "hst"),
    )
    out_specs = (
        P(TBL, "hst"),
        P(TBL, "hst", None, None),
        P(TBL, "hst", None),
        P(TBL, "hst", None, None, None),
        P(TBL, "hst", None, None),
    )
    return jax.shard_map(
        on_device, mesh=torus, in_specs=in_specs, out_specs=out_specs, check_vma=False
    )
```

```python
import functools

import jax
import jax.numpy as jnp
from jax import lax
from jax.experimental import pallas as pl
from jax.experimental.pallas import tpu as pltpu
from jax.sharding import Mesh
from jax.sharding import PartitionSpec as P

TBL = ("tbl_0", "tbl_1", "tbl_2")
Z, X, C, H = "tbl_0", "tbl_1", "tbl_2", "hst"

LEARN_RATE = 0.05
EPSILON = 1e-08
F32 = jnp.float32
BF16 = jnp.bfloat16
I32 = jnp.int32
VMEM = pl.BlockSpec(memory_space=pltpu.VMEM)
SMEM = pl.BlockSpec(memory_space=pltpu.SMEM)
MOST = 128
HELD = 136


def shifted(x, axis, step):
    size = lax.axis_size(axis)
    return lax.ppermute(x, axis, [(i, (i + step) % size) for i in range(size)])


def call(body, ins, outs, scratch, flops, moved, name, limit=20):
    return pl.pallas_call(
        body,
        in_specs=ins,
        out_specs=[VMEM] * len(outs),
        out_shape=outs,
        scratch_shapes=scratch,
        compiler_params=pltpu.CompilerParams(vmem_limit_bytes=limit << 20),
        cost_estimate=pl.CostEstimate(flops=flops, bytes_accessed=moved, transcendentals=0),
        name=name,
    )


def top_kernel(pos, pooled, w_up, grad_out, delta, own, one, two, three, feature):
    width = 256

    def column(i, carry):
        at = pl.ds(pl.multiple_of(i * width, width), width)
        preact = jnp.dot(pooled[...], w_up[:, at], preferred_element_type=F32)
        s = jax.nn.sigmoid(preact)
        delta[:, at] = (grad_out[:, at].astype(F32) * s * (1.0 + preact * (1.0 - s))).astype(BF16)
        return carry

    lax.fori_loop(0, 4, column, 0)
    h = pos[3]

    def part(k, carry):
        row = pl.multiple_of(lax.rem(h + k, 4) * width, width)
        feature[k] = lax.dot_general(
            delta[...],
            w_up[pl.ds(row, width), :],
            (((1,), (1,)), ((), ())),
            preferred_element_type=F32,
        )
        return carry

    lax.fori_loop(0, 4, part, 0)
    bags = delta.shape[0]
    for k, ref in enumerate((own, one, two, three)):
        for t in range(2):
            ref[t * bags : (t + 1) * bags, :] = feature[k, :, t * 128 : (t + 1) * 128].astype(ref.dtype)


def field_kernel(owner, row, weight, lens, out, earlier_out):
    tables, bag, bags = owner.shape
    for t in range(tables):
        slot = lax.broadcasted_iota(I32, (bag, bags), 0)
        used = jnp.where(slot < lens[t : t + 1, :], owner[t], 64)
        fields = [used, lax.shift_right_logical(row[t], 2), row[t] & 3]
        fields = [f.astype(F32) for f in fields] + [weight[t].astype(F32)]
        fields = jnp.concatenate(fields, axis=0).astype(BF16)
        for q in range(4):
            out[t, q * 32 : (q + 1) * 32, :] = fields[:, q * 128 : (q + 1) * 128]
    shape = earlier_out.shape
    earlier = lax.broadcasted_iota(I32, shape, 0) < lax.broadcasted_iota(I32, shape, 1)
    earlier_out[...] = jnp.where(earlier, 1.0, 0.0).astype(BF16)


def own_kernel(own, one, two, three, fields, out):
    bags, lines = own.shape[0] // 2, fields.shape[1]
    for t in range(2):
        at = slice(t * bags, (t + 1) * bags)
        total = own[at, :] + one[at, :].astype(F32) + two[at, :].astype(F32) + three[at, :].astype(F32)
        first = t * (bags + lines)
        out[first : first + bags, :] = total.astype(BF16)
        out[first + bags : first + bags + lines, :] = fields[t]


STEPS = (1, 2, 2, 2, 1)


def pick_kernel(count, pos, earlier, *refs):
    blocks = 2 if count == 2 or len(refs) == 19 else 1
    msgs, refs = refs[:blocks], refs[blocks:]
    outs, (bag_all, dense, ranks, picks, rhs) = refs[:12], refs[12:]
    bags = bag_all.shape[2]
    units = 2 * count
    lines = 128
    z, x, c = pos[0], pos[1], pos[2]
    j = lax.broadcasted_iota(I32, (8, bags), 0)
    ids = (z * 8 + 2 * ((x + j) & 3) + ((c + (j >> 2)) & 1)).astype(F32)
    for s in range(count):
        for t in range(2):
            if count == 2:
                ref, first = msgs[s], t * (bags + lines)
            elif blocks == 2:
                ref, first = msgs[t], 0
            else:
                ref, first = msgs[0], t * (bags + lines)
            bag_all[s, t] = ref[first : first + bags, :]
            first += bags
            fields = jnp.concatenate(
                [ref[first + q * 32 : first + (q + 1) * 32, :].astype(F32) for q in range(4)], axis=1
            )
            high = jnp.zeros((8, bags), F32)
            low, weight = high, high
            for l in range(8):
                mine = fields[l : l + 1] == ids
                high = high + jnp.where(mine, fields[8 + l : 9 + l], 0.0)
                low = low + jnp.where(mine, fields[16 + l : 17 + l], 0.0)
                weight = weight + jnp.where(mine, fields[24 + l : 25 + l], 0.0)
            u = 2 * s + t
            dense[u, 0:8] = high
            dense[u, 8:16] = weight
            dense[u, 16:24] = low
    present = jnp.concatenate([dense[u, 8:16] for u in range(units)], axis=0) > 0.0
    rank = jnp.dot(
        jnp.where(present, 1.0, 0.0).astype(BF16), earlier[...], preferred_element_type=F32
    )
    rank = jnp.where(present, rank, 255.0)
    for u in range(units):
        ranks[u] = rank[8 * u : 8 * u + 8]
    place = lax.broadcasted_iota(I32, (MOST, bags), 0).astype(F32).astype(BF16)

    def source(s, carry):
        for t in range(2):
            u = 2 * s + t
            rhs[t, :, :128] = bag_all[s, t]
            moved = jnp.concatenate([dense[u], jnp.zeros((128 - 24, bags), F32)], axis=0)
            rhs[t, :, 128:] = moved.T.astype(BF16)
            rank = ranks[u].astype(BF16)
            for o in range(8):
                line = jnp.broadcast_to(rank[o : o + 1, :], (MOST, bags))
                picks[t, o * MOST : (o + 1) * MOST, :] = jnp.where(
                    line == place, jnp.ones((), BF16), jnp.zeros((), BF16)
                )
        for t in range(2):
            for o in range(0, 8, 2):
                got2 = jnp.dot(
                    picks[t, o * MOST : (o + 2) * MOST, :], rhs[t], preferred_element_type=F32
                )
                for i in range(2):
                    q = o + i
                    got = got2[i * MOST : (i + 1) * MOST]
                    rows, low, meta = outs[3 * (2 * t + q // 4) : 3 * (2 * t + q // 4) + 3]
                    k = q % 4
                    rows[s, k] = got[:, :128].astype(BF16)
                    low[s, k] = jnp.broadcast_to(
                        got[:, 128 + 16 + q : 128 + 17 + q], (MOST, 128)
                    ).astype(BF16)
                    side = got[:, 128:].T
                    meta[s, k : k + 1, :] = side[q : q + 1]
                    meta[s, 4 + k : 5 + k, :] = side[8 + q : 9 + q]
        return carry

    lax.fori_loop(0, count, source, 0)


def spread_one(k, steps, onto, both):
    ids = lax.broadcasted_iota(I32, (256, MOST), 0).astype(F32).astype(BF16)
    s = 0
    for rows, low, meta in steps:
        for i in range(rows.shape[0]):
            at = slice(s * MOST, (s + 1) * MOST)
            high = jnp.broadcast_to(meta[i, pl.ds(k, 1), :].astype(BF16), (256, MOST))
            wt = jnp.broadcast_to(meta[i, pl.ds(k + 4, 1), :].astype(BF16), (256, MOST))
            onto[:, at] = jnp.where(high == ids, wt, jnp.zeros((), BF16))
            vec, bits = rows[i, k], low[i, k]
            for l in range(4):
                both[at, l * 128 : (l + 1) * 128] = jnp.where(
                    bits == jnp.full((), l, BF16), vec, jnp.zeros((), BF16)
                )
            s += 1
    return jnp.dot(onto[...], both[...], preferred_element_type=F32)


def send_kernel(*refs):
    steps = [refs[3 * i : 3 * i + 3] for i in range(5)]
    out, onto, both = refs[15:]

    def one(k, carry):
        out[k] = spread_one(k, steps, onto, both).astype(BF16)
        return carry

    lax.fori_loop(0, 4, one, 0)


def keep_kernel(other0, other1, *refs):
    outs, onto, both, total = refs[30:34], refs[34], refs[35], refs[36]
    for t, other in enumerate((other0, other1)):
        steps = [refs[15 * t + 3 * i : 15 * t + 3 * i + 3] for i in range(5)]

        def one(k, carry):
            total[k] = spread_one(k, steps, onto, both) + other[k].astype(F32)
            return carry

        lax.fori_loop(0, 4, one, 0)
        for k in range(4):
            outs[k][t * 256 : (t + 1) * 256, :] = total[k].astype(outs[k].dtype)


def grad_kernel(pos, pooled, delta, keep, send, half):
    x, c = pos[1], pos[2]

    def piece(i, carry):
        at = pl.ds(pl.multiple_of(i * 512, 512), 512)
        half[...] = lax.dot_general(
            pooled[:, at], delta[...], (((0,), (0,)), ((), ())), preferred_element_type=F32
        )
        for j in range(4):
            kz = i * 4 + j
            for k in range(4):
                row = j * 128 + lax.rem(x + k, 4) * 32
                keep[k, kz] = half[pl.ds(pl.multiple_of(row + c * 16, 16), 16), :]
                send[k, kz] = half[pl.ds(pl.multiple_of(row + (1 - c) * 16, 16), 16), :]
        return carry

    lax.fori_loop(0, 2, piece, 0)


def finish_kernel(pos, total, blocks, out):
    z = pos[0]
    acc = total[z]
    for k in range(1, 8):
        acc = acc + blocks[lax.rem(z + k, 8)].astype(F32)
    out[...] = acc


def leave_kernel(slots_s, goal_s, accum_s, weight, out):
    slot_out, weight_out, accum_out = (out.at[i] for i in range(3))
    slot_out[...] = jnp.full(slot_out.shape, -1.0, F32)
    weight_out[...] = jnp.zeros(slot_out.shape, F32)
    accum_out[...] = jnp.zeros(slot_out.shape, F32)

    def leave(i, carry):
        for j in range(4):
            slot, goal = slots_s[4 * i + j], goal_s[4 * i + j]
            at = pl.ds(goal, 1)
            slot_out[at, :] = jnp.full((1, 128), slot, I32).astype(F32)
            weight_out[at, :] = weight[pl.ds(slot, 1), :]
            accum_out[at, :] = jnp.full((1, 128), accum_s[slot], F32)
        return carry

    lax.fori_loop(0, slots_s.shape[0] // 4, leave, 0)


def square():
    return lax.broadcasted_iota(I32, (128, 128), 0) == lax.broadcasted_iota(I32, (128, 128), 1)


def evict_kernel(slot_map, leaving, *refs):
    slot_in, weight, accum = (leaving.at[i] for i in range(3))
    parts, rhs, held, pick, sums = refs[:4], refs[4], refs[5:9], refs[9], refs[10]
    for t in range(2):
        at = slice(t * 256, (t + 1) * 256)
        own = parts[0][at, :].astype(F32)
        for k in range(1, 4):
            own = own + parts[k][at, :].astype(F32)
        high = own.astype(BF16)
        low = (own - high.astype(F32)).astype(BF16)
        for l in range(4):
            at = (4 * t + l) * 256
            rhs[at : at + 256, :128] = high[:, l * 128 : (l + 1) * 128]
            rhs[at : at + 256, 128:] = low[:, l * 128 : (l + 1) * 128]
    eye = square()
    for i in range(16):
        lane = slice(i * 128, (i + 1) * 128)
        pick[:, lane] = jnp.where(slot_in[:512, :] == slot_map[:, lane], 1.0, 0.0).astype(BF16)
    sums[...] = jnp.dot(pick[...], rhs[...], preferred_element_type=F32)
    for i in range(4):
        at = slice(i * 128, (i + 1) * 128)
        g = sums[at, :128] + sums[at, 128:]
        acc = accum[at, :] + jnp.sum(g * g, axis=1, keepdims=True) * (1.0 / 128.0)
        held[i][:128, :] = weight[at, :] - LEARN_RATE * g / (jnp.sqrt(acc) + EPSILON)
        line = jnp.sum(jnp.where(eye, acc, 0.0), axis=0, keepdims=True)
        held[i][128:, :] = jnp.broadcast_to(line, (HELD - 128, 128))


def update_kernel(slot_map, rhs, weight, accum, new_weight, new_accum, pick, sums):
    eye = square()
    step, part = 512, 256
    ids = lax.broadcasted_iota(I32, (part, 2048), 0).astype(F32).astype(BF16)
    slot_row = slot_map[...]

    def chunk(i, carry):
        at = pl.multiple_of(i * step, step)
        for j in range(step // part):
            near = slot_row - (at + j * part).astype(F32)
            near = jnp.where((near >= 0.0) & (near < part), near, 2.0 * part).astype(BF16)
            pick[j * part : (j + 1) * part, :] = jnp.where(
                jnp.broadcast_to(near, (part, 2048)) == ids, jnp.ones((), BF16), jnp.zeros((), BF16)
            )
        sums[...] = jnp.dot(pick[...], rhs[...], preferred_element_type=F32)
        for j in range(step // 128):
            part_at = slice(j * 128, (j + 1) * 128)
            g = sums[part_at, :128] + sums[part_at, 128:]
            b = i * (step // 128) + j
            kept = jnp.sum(jnp.where(eye, accum[pl.ds(b, 1), :], 0.0), axis=1, keepdims=True)
            acc = kept + jnp.sum(g * g, axis=1, keepdims=True) * (1.0 / 128.0)
            here = pl.ds(pl.multiple_of(at + j * 128, 128), 128)
            new_accum[pl.ds(b, 1), :] = jnp.sum(jnp.where(eye, acc, 0.0), axis=0, keepdims=True)
            new_weight[here, :] = weight[here, :] - LEARN_RATE * g / (jnp.sqrt(acc) + EPSILON)
        return carry

    lax.fori_loop(0, 2048 // step, chunk, 0)


def arrive_kernel(pos, b0, b1, b2, b3, rows, accum):
    h = pos[3]
    for k, ref in enumerate((b0, b1, b2, b3)):
        at = lax.rem(h + 4 - k, 4)
        rows[at] = ref[:128, :]
        accum[pl.ds(at, 1), :] = ref[128:129, :]


def together(*groups):
    flat = [a for g in groups for a in g]
    flat = lax.optimization_barrier(flat)
    out = []
    for g in groups:
        out.append(flat[: len(g)])
        flat = flat[len(g) :]
    return out


def on_device(
    pooled,
    w_up,
    grad_out,
    owners,
    rows,
    lookup_weight,
    lens,
    slot_map,
    cache_weight,
    cache_accum,
    evict_slots,
    evict_dest,
    evict_count,
):
    shape = jax.ShapeDtypeStruct
    bags = pooled.shape[0]
    z, x, c, h = (lax.axis_index(a) for a in (Z, X, C, H))
    pos = jnp.stack([z, x, c, h]).astype(I32)

    delta, *parts = call(
        top_kernel,
        [SMEM, VMEM, VMEM, VMEM],
        [shape((bags, 1024), BF16), shape((2 * bags, 128), F32)] + [shape((2 * bags, 128), BF16)] * 3,
        [pltpu.VMEM((4, bags, 256), F32)],
        2 << 30,
        6 << 20,
        "top",
        60,
    )(pos, pooled, w_up, grad_out)
    got = [shifted(parts[k], H, k) for k in (1, 2, 3)]

    (delta,), (owners, rows, lookup_weight, lens) = together(
        (delta,), (owners, rows, lookup_weight, lens)
    )
    fields, earlier = call(
        field_kernel,
        [VMEM] * 4,
        [shape((2, 128, 128), BF16), shape((bags, bags), BF16)],
        [],
        1 << 20,
        1 << 20,
        "fields",
    )(*[jnp.swapaxes(a, 1, 2) for a in (owners, rows, lookup_weight)], lens)
    (own,) = call(
        own_kernel, [VMEM] * 5, [shape((2 * (bags + 128), 128), BF16)], [], 1 << 20, 2 << 20, "own"
    )(parts[0], *got, fields)

    def pick(step, blocks):
        count = STEPS[step]
        outs = [
            shape((count, 4, MOST, 128), BF16),
            shape((count, 4, MOST, 128), BF16),
            shape((count, 8, 128), F32),
        ] * 4
        return call(
            functools.partial(pick_kernel, count),
            [SMEM, VMEM] + [VMEM] * len(blocks),
            outs,
            [
                pltpu.VMEM((count, 2, bags, 128), BF16),
                pltpu.VMEM((2 * count, 24, bags), F32),
                pltpu.VMEM((2 * count, 8, bags), F32),
                pltpu.VMEM((2, 8 * MOST, bags), BF16),
                pltpu.VMEM((2, bags, 256), BF16),
            ],
            1 << 30,
            4 << 20,
            f"pick{step}",
        )(pos, earlier, *blocks)

    up, down = shifted(own, Z, 1), shifted(own, Z, -1)
    (delta,), (own,) = together((delta,), (own,))
    grad, there = call(
        grad_kernel,
        [SMEM, VMEM, VMEM],
        [shape((4, 8, 16, 1024), F32)] * 2,
        [pltpu.VMEM((512, 1024), F32)],
        1 << 30,
        6 << 20,
        "grad",
    )(pos, pooled, delta)
    near = (up, down)
    picked = [pick(0, (own,))]
    near, (grad, there), picked[0] = together(near, (grad, there), picked[0])
    up, down = near
    there = shifted(there, C, 1)
    mid = (shifted(up, Z, 1), shifted(down, Z, -1))
    grad_x = grad + there
    total, blocks = grad_x[0], [grad_x[k].astype(BF16) for k in (1, 2, 3)]
    early = pick(1, near)
    mid, near, (total,), blocks, early = together(mid, near, (total,), blocks, early)
    up, down = mid
    got_x = [shifted(blocks[k - 1], X, k) for k in (1, 2, 3)]
    far = (shifted(up, Z, 1), shifted(down, Z, -1))
    picked.append(early)
    picked.append(pick(2, mid))
    far, picked[1], picked[2] = together(far, picked[1], picked[2])
    up, down = far
    part = bags + 128
    last = (shifted(up[:part], Z, 1), shifted(down[part:], Z, -1))
    picked.append(pick(3, far))
    last, got_x, picked[3] = together(last, got_x, picked[3])
    picked.append(pick(4, last))

    work = [pltpu.VMEM((256, 8 * MOST), BF16), pltpu.VMEM((8 * MOST, 512), BF16)]
    half = lambda t, side: [a for p in picked for a in p[3 * (2 * t + side) : 3 * (2 * t + side) + 3]]
    others = []
    for t in range(2):
        if others:
            others, picked[4] = together(others, picked[4])
        (out,) = call(
            send_kernel, [VMEM] * 15, [shape((4, 256, 512), BF16)], work, 4 << 30, 5 << 20, f"send{t}"
        )(*half(t, 1))
        others.append(out)
    others = [shifted(out, C, 1) for out in others]
    outs = call(
        keep_kernel,
        [VMEM] * 32,
        [shape((512, 512), BF16)] * 4,
        work + [pltpu.VMEM((4, 256, 512), F32)],
        8 << 30,
        10 << 20,
        "keep",
    )(*others, *half(0, 0), *half(1, 0))
    arrived = [outs[0]] + [shifted(outs[k], X, k) for k in (1, 2, 3)]

    for block in got_x:
        total = total + block.astype(F32)
    first, total, slot_map, evict_slots, evict_dest = lax.optimization_barrier(
        (arrived[0], total, slot_map, evict_slots, evict_dest)
    )
    arrived[0] = first
    list_len = evict_slots.shape[-1]
    departure = evict_dest[0, 0]
    list_ids = jnp.arange(list_len, dtype=I32)
    live = list_ids < evict_count[0, 0]
    picks = ((departure[:, None] == jnp.arange(4, dtype=I32)) & live[:, None]).astype(BF16)
    before = (list_ids[:, None] > list_ids[None, :]).astype(BF16)
    counted = jnp.dot(before, picks, preferred_element_type=F32)
    placed = jnp.sum(counted * picks.astype(F32), axis=-1).astype(I32)
    goal = jnp.where(live, lax.rem(departure + 4 - h, 4) * 128 + placed, 512)
    slot_rows = jnp.swapaxes(slot_map.reshape(2, 256, 4), 1, 2).reshape(1, 2048).astype(F32)
    slot_rows, goal = lax.optimization_barrier((slot_rows, goal))
    leaving = call(
        leave_kernel,
        [SMEM] * 3 + [VMEM],
        [shape((3, 520, 128), F32)],
        [],
        1 << 10,
        1 << 20,
        "leave",
    )(evict_slots.reshape(-1), goal, cache_accum.reshape(-1), cache_weight[0, 0])
    (total,), _ = together((total,), leaving)
    blocks = lax.all_to_all(total.astype(BF16), Z, split_axis=0, concat_axis=0, tiled=True)
    (grad_up,) = call(
        finish_kernel,
        [SMEM, VMEM, VMEM],
        [shape((16, 1024), F32)],
        [],
        1 << 10,
        1 << 18,
        "finish",
    )(pos, total, blocks)
    rhs, *held = call(
        evict_kernel,
        [VMEM] * 6,
        [shape((2048, 256), BF16)] + [shape((HELD, 128), F32)] * 4,
        [pltpu.VMEM((512, 2048), BF16), pltpu.VMEM((512, 256), F32)],
        1 << 29,
        4 << 20,
        "evict",
    )(slot_rows, *leaving, *arrived)
    moved = [shifted(held[k], H, k) for k in (1, 2, 3)]
    new_weight, new_accum = call(
        update_kernel,
        [VMEM] * 4,
        [shape((2048, 128), F32), shape((16, 128), F32)],
        [pltpu.VMEM((512, 2048), BF16), pltpu.VMEM((512, 256), F32)],
        2 << 30,
        4 << 20,
        "update",
    )(slot_rows, rhs, cache_weight[0, 0], cache_accum.reshape(16, 128))
    held = [held[0]] + moved
    held_rows, held_accum = call(
        arrive_kernel,
        [SMEM] + [VMEM] * 4,
        [shape((4, 128, 128), F32), shape((4, 128), F32)],
        [],
        1 << 10,
        1 << 19,
        "arrive",
    )(pos, *held)
    return (
        grad_up,
        new_weight[None, None],
        new_accum.reshape(1, 1, 2048),
        held_rows[None, None],
        held_accum[None, None],
    )


def solution(mesh):
    torus = Mesh(mesh.devices.reshape(8, 4, 2, mesh.shape["hst"]), (Z, X, C, H))
    in_specs = (
        P(TBL, None),
        P(None, "hst"),
        P(TBL, "hst"),
        P("hst", TBL, None),
        P("hst", TBL, None),
        P("hst", TBL, None),
        P("hst", TBL),
        P(TBL, "hst", None),
        P(TBL, "hst", None, None),
        P(TBL, "hst", None),
        P(TBL, "hst", None),
        P(TBL, "hst", None),
        P(TBL, "hst"),
    )
    out_specs = (
        P(TBL, "hst"),
        P(TBL, "hst", None, None),
        P(TBL, "hst", None),
        P(TBL, "hst", None, None, None),
        P(TBL, "hst", None, None),
    )
    return jax.shard_map(
        on_device, mesh=torus, in_specs=in_specs, out_specs=out_specs, check_vma=False
    )
```
